32 devices in a mesh: pipe: 4 (over y, core), band: 8 (over z, x).
Axes of the slice: x: 2, y: 2, z: 4, core: 2. Of those that a mesh axis runs over, the one named last changes fastest.
Arguments:
- memory: float32 [4, 512, 512, 128], P('pipe', 'band'), may hold values from -6 to 6
- shear_blocks: bfloat16 [4, 3, 4, 4, 2, 128, 128], P('pipe'), may hold values from -0.375 to 0.375
- shear_offsets: int32 [4, 3, 4], P('pipe'), may hold values from 0 to 3
- block_lists: int32 [4, 3, 4, 2], P('pipe'), may hold values from 0 to 3
- mix_weight: bfloat16 [4, 128, 128], P('pipe'), may hold values from -0.5 to 0.5
Outputs:
- memory_out: float32 [4, 512, 512, 128], P('pipe', 'band')
The draws below stay inside these ranges and needn't reach their ends.
All inputs are finite; a program needn't handle non-finite values.
Results may differ from the reference program's by a relative error of at most 0.008.
Values may be sent and summed in bfloat16 or wider, within the bound.
No kernel may reach another device: no remote copies, remote signals or barrier semaphores. Data moves between devices by JAX's collectives and lax.ppermute only.
A program may use at most 192 MiB of HBM per device.

```python
import jax
import jax.numpy as jnp
from jax import lax

GRID = 512
C = 128
BLK = 128
NBAND = 2
TICKS = 2
QB = 4
SECTIONS = 4


def with_ends(values, own_key, low, high):
    longest = values.shape.index(max(values.shape))
    spots = []
    for shift in (0, 1):
        where = [jax.random.randint(jax.random.fold_in(own_key, axis), (), 0, length) for axis, length in enumerate(values.shape)]
        where[longest] = (where[longest] + shift) % values.shape[longest]
        spots.append(tuple(where))
    return values.at[spots[0]].set(low).at[spots[1]].set(high)


def levels(key, extent, shards, least, high):
    level, own = 1.0, jax.random.fold_in(key, 6)
    for axis_at, parts in shards:
        heights = jnp.exp(jax.random.uniform(jax.random.fold_in(own, axis_at), (parts,), jnp.float32, least / len(shards), high / len(shards)))
        level = level * jnp.repeat(heights, extent[axis_at] // parts).reshape([-1 if axis == axis_at else 1 for axis in range(len(extent))])
    return level


def normal_values(stream_key, dims, scale, reach, shards=(), held_as=jnp.bfloat16):
    factor_of = levels(stream_key, dims, shards, -0.22, 0.18) if shards else 1.0
    entries = jax.random.normal(stream_key, dims, jnp.float32) * scale * factor_of
    return jnp.minimum(jnp.maximum(entries, -reach), reach).astype(held_as)


def setup_inputs(seed: int = 0) -> dict:
    key_of = jax.random.split(jax.random.key(seed), 6)
    memory = normal_values(key_of[0], (SECTIONS, GRID, GRID, C), 1.0, 6.0, ((0, 4), (1, 8)), jnp.float32)
    shear_blocks = normal_values(key_of[1], (SECTIONS, 3, QB, QB, NBAND, BLK, BLK), (NBAND * BLK) ** -0.5, 0.375, ((0, 4),))
    shear_offsets = with_ends(jax.random.randint(key_of[2], (SECTIONS, 3, QB), 0, QB), jax.random.fold_in(key_of[2], 1), 0, QB - 1).astype(jnp.int32)
    block_lists = with_ends(jax.random.randint(key_of[3], (SECTIONS, 3, QB, NBAND), 0, QB), jax.random.fold_in(key_of[3], 1), 0, QB - 1).astype(jnp.int32)
    mix_weight = normal_values(key_of[4], (SECTIONS, C, C), C ** -0.5, 0.5, ((0, 4),))
    return dict(memory=memory, shear_blocks=shear_blocks, shear_offsets=shear_offsets, block_lists=block_lists, mix_weight=mix_weight)


def shear_rows(values, weights, offsets, list_table):
    line_count = values.shape[0] // BLK
    shifted = (jnp.arange(QB, dtype=jnp.int32)[None, :, None] + offsets[:, None, None] + list_table[None]) % QB
    blocked = values.reshape(line_count, BLK, QB, BLK, C)

    def pick(section_part, source_blocks):
        return section_part[:, source_blocks]

    picked = jax.vmap(pick)(blocked, shifted.astype(jnp.int32))
    output = jnp.einsum("iqtab,irqtbc->irqac", weights.astype(jnp.float32), picked.astype(jnp.float32))
    return output.reshape(values.shape)


def section(arguments):
    memory_state, blocks, offsets, list_table, mixing = arguments
    rounded = memory_state.astype(jnp.bfloat16)
    sheared_one = shear_rows(rounded, blocks[0], offsets[0], list_table[0]).astype(jnp.bfloat16)
    turned = jnp.swapaxes(sheared_one, 0, 1)
    sheared_two = jnp.swapaxes(shear_rows(turned, blocks[1], offsets[1], list_table[1]), 0, 1).astype(jnp.bfloat16)
    sheared_three = shear_rows(sheared_two, blocks[2], offsets[2], list_table[2]).astype(jnp.bfloat16)
    mixed_term = jnp.dot(sheared_three.reshape(-1, C), mixing, preferred_element_type=jnp.float32)
    return memory_state + mixed_term.reshape(memory_state.shape)


def reference(memory, shear_blocks, shear_offsets, block_lists, mix_weight):
    memory_state = memory
    for window_step in range(TICKS):
        result = lax.map(section, (memory_state, shear_blocks, shear_offsets, block_lists, mix_weight))
        memory_state = jnp.roll(result, 1, axis=0)
    return memory_state
```

```python
import jax
import jax.numpy as jnp
from jax import lax
from jax.experimental import pallas as pl
from jax.experimental.pallas import tpu as pltpu
from jax.sharding import Mesh, PartitionSpec as P

TICKS = 2
CHANNEL_CHUNKS = 4
ROW_TILE = 16
AXES = ("lane", "core", "half", "rest")
GROUP = ("core", "rest")
VMEM = pltpu.CompilerParams(vmem_limit_bytes=58 << 20)


def whole(shape):
    return pl.BlockSpec(shape, lambda *_: (0,) * len(shape))


def turn(memory, parts, members):
    rows, width, channels = memory.shape
    each = channels // members // parts

    def body(source, *outs):
        turned = jnp.transpose(source[...].astype(jnp.bfloat16), (2, 0, 1))
        split = turned.reshape(members, parts, each, ROW_TILE, width)
        for part in range(parts):
            outs[part][...] = split[:, part]

    return pl.pallas_call(
        body,
        grid=(rows // ROW_TILE,),
        in_specs=[pl.BlockSpec((ROW_TILE, width, channels), lambda i: (i, 0, 0))],
        out_specs=[pl.BlockSpec((members, each, ROW_TILE, width), lambda i: (0, 0, i, 0))] * parts,
        out_shape=[jax.ShapeDtypeStruct((members, each, rows, width), jnp.bfloat16)] * parts,
        compiler_params=VMEM,
        name="turn",
    )(memory)


def dense(blocks, table, which, shear, transposed):
    lines, outs_count, slots, wide = blocks.shape[2:6]
    size = outs_count * wide

    def body(table_ref, which_ref, source, out):
        line = pl.program_id(0)
        out[...] = jnp.zeros(out.shape, out.dtype)
        for q in range(outs_count):
            for t in range(slots):
                place = table_ref[((which_ref[0] * 3 + shear) * lines + line) * outs_count * slots + q * slots + t]
                start = pl.multiple_of(place * wide, wide)
                block = source[0, 0, 0, q, t]
                fixed = pl.ds(q * wide, wide)
                moved = pl.ds(start, wide)
                if transposed:
                    out[0, moved, fixed] += block.T
                else:
                    out[0, fixed, moved] += block

    return pl.pallas_call(
        body,
        grid_spec=pltpu.PrefetchScalarGridSpec(
            num_scalar_prefetch=2,
            grid=(lines,),
            in_specs=[
                pl.BlockSpec(
                    (1, 1, 1, outs_count, slots, wide, wide),
                    lambda i, table_ref, which_ref: (which_ref[0], shear, i, 0, 0, 0, 0),
                )
            ],
            out_specs=pl.BlockSpec((1, size, size), lambda i, *_: (i, 0, 0)),
        ),
        out_shape=jax.ShapeDtypeStruct((lines, size, size), jnp.bfloat16),
        compiler_params=VMEM,
        name="dense",
    )(table, which, blocks)


def sheared(values, first, second, third, targets, part):
    members, each, rows, width = values.shape
    lines = first.shape[0]
    wide = width // lines
    per = wide // rows
    pair = 2 if each % 2 == 0 else 1
    by_rows = targets is not None
    count = rows // ROW_TILE if by_rows else 1

    def body(source, first_ref, second_ref, third_ref, *refs):
        outs, (one, two) = refs[-2 - count : -2], refs[-2:]
        for ch in range(pair):
            for i in range(lines):
                lhs = source[per * i : per * (i + 1), ch].reshape(wide, width)
                got = jnp.dot(lhs, first_ref[i], preferred_element_type=jnp.float32).astype(jnp.bfloat16)
                for j in range(lines):
                    one[j, i * wide : (i + 1) * wide, ch * wide : (ch + 1) * wide] = got[:, j * wide : (j + 1) * wide]
        for j in range(lines):
            got = jnp.dot(second_ref[j], one[j], preferred_element_type=jnp.float32).astype(jnp.bfloat16)
            for ch in range(pair):
                two[ch, :, j * wide : (j + 1) * wide] = got[:, ch * wide : (ch + 1) * wide]
        for ch in range(pair):
            for i in range(lines):
                lhs = two[ch, i * wide : (i + 1) * wide]
                got = jnp.dot(lhs, third_ref[i], preferred_element_type=jnp.float32).astype(jnp.bfloat16)
                split = got.reshape(per, count, rows // count, width)
                for r in range(count):
                    outs[r][per * i : per * (i + 1), ch] = split[:, r]

    steps = each // pair
    out_each = targets[0].shape[1] if by_rows else each
    base = part * steps if by_rows else 0
    given = [t for t in targets if t is not None] if by_rows and part else []
    out_rows = rows // count
    return pl.pallas_call(
        body,
        grid=(steps,),
        in_specs=[pl.BlockSpec((members, pair, rows, width), lambda c: (0, c, 0, 0))]
        + [whole(first.shape)] * 3
        + [pl.BlockSpec(memory_space=pl.ANY)] * len(given),
        out_specs=[pl.BlockSpec((members, pair, out_rows, width), lambda c: (0, base + c, 0, 0))] * count,
        out_shape=[jax.ShapeDtypeStruct((members, out_each, out_rows, width), jnp.bfloat16)] * count,
        scratch_shapes=[
            pltpu.VMEM((lines, width, pair * wide), jnp.bfloat16),
            pltpu.VMEM((pair, width, width), jnp.bfloat16),
        ],
        input_output_aliases={4 + r: r for r in range(len(given))},
        compiler_params=VMEM,
        name="sheared",
    )(values, first, second, third, *given)


def joined(refs, members):
    return jnp.concatenate([ref[j] for j in range(members) for ref in refs], axis=0)


def mixed(fields, state, mixing):
    parts = len(fields)
    members, each, rows, width = fields[0].shape
    channels = mixing.shape[0]

    def body(*refs):
        mix = refs[2 * parts][...]
        outs = refs[2 * parts + 1 :]
        turned = jnp.swapaxes(joined(refs[:parts], members), 0, 1)
        got = [
            lax.dot_general(mix, turned[l], (((0,), (0,)), ((), ())), preferred_element_type=jnp.float32)
            for l in range(ROW_TILE)
        ]
        back = jnp.swapaxes(jnp.stack([g.astype(jnp.bfloat16) for g in got], 0), 0, 1)
        split = back.reshape(members, parts, each, ROW_TILE, width)
        for k in range(parts):
            total = refs[parts + k][...].astype(jnp.float32) + split[:, k].astype(jnp.float32)
            outs[k][...] = total.astype(jnp.bfloat16)

    block = pl.BlockSpec((members, each, ROW_TILE, width), lambda i: (0, 0, i, 0))
    return pl.pallas_call(
        body,
        grid=(rows // ROW_TILE,),
        in_specs=[block] * (2 * parts) + [whole((channels, channels))],
        out_specs=[block] * parts,
        out_shape=[jax.ShapeDtypeStruct(fields[0].shape, jnp.bfloat16)] * parts,
        compiler_params=VMEM,
        name="mixed",
    )(*fields, *state, mixing)


def finished(field, state, mixing, row_chunk):
    channels, rows, width = field.shape
    parts = len(state)
    members, each = state[0].shape[:2]
    piece = min(width, 128)

    def body(*refs):
        mix = refs[1 + parts][...]
        out = refs[2 + parts]
        turned = jnp.swapaxes(refs[0][...], 0, 1)
        old = jnp.swapaxes(joined(refs[1 : 1 + parts], members), 0, 1)
        for l in range(rows):
            got = lax.dot_general(mix, turned[l], (((0,), (0,)), ((), ())), preferred_element_type=jnp.float32)
            out[l] = (got + old[l].astype(jnp.float32)).astype(jnp.bfloat16).T

    return pl.pallas_call(
        body,
        grid=(width // piece,),
        in_specs=[pl.BlockSpec((channels, rows, piece), lambda i: (0, 0, i))]
        + [pl.BlockSpec((members, each, rows, piece), lambda i: (0, 0, row_chunk, i))] * parts
        + [whole((channels, channels))],
        out_specs=pl.BlockSpec((rows, piece, channels), lambda i: (0, i, 0)),
        out_shape=jax.ShapeDtypeStruct((rows, width, channels), jnp.bfloat16),
        compiler_params=VMEM,
        name="finished",
    )(field, *state, mixing)


def placed(rows_in, target, row_chunk, shape):
    rows, width, channels = rows_in.shape
    piece = min(width, 128)

    def body(source, *refs):
        refs[-1][...] = source[...].astype(jnp.float32)

    given = [] if target is None else [target]
    return pl.pallas_call(
        body,
        grid=(width // piece,),
        in_specs=[pl.BlockSpec((rows, piece, channels), lambda i: (0, i, 0))]
        + [pl.BlockSpec(memory_space=pl.ANY)] * len(given),
        out_specs=pl.BlockSpec((rows, piece, channels), lambda i: (row_chunk, i, 0)),
        out_shape=jax.ShapeDtypeStruct(shape, jnp.float32),
        input_output_aliases={1: 0} if given else {},
        compiler_params=VMEM,
        name="placed",
    )(rows_in, *given)


def exchanged(values):
    return lax.all_to_all(values, GROUP, split_axis=0, concat_axis=0, tiled=True)


def solution(mesh):
    sections = mesh.shape["pipe"]
    bands = mesh.shape["band"]
    lanes, rest = sections // 2, bands // 2
    fine = Mesh(mesh.devices.reshape(lanes, 2, 2, rest), AXES)

    def flat(pipe, half, place):
        return (pipe * 2 + half) * rest + place

    gather_route = []
    return_route = []
    for lane in range(lanes):
        for core in range(2):
            for half in range(2):
                for place in range(rest):
                    here = flat(lane * 2 + core, half, place)
                    gather_route.append((here, flat(lane * 2 + half, core, place)))
                    owner = (lane * 2 + half + TICKS) % sections
                    return_route.append((here, flat(owner, core, place)))

    def on_device(memory, shear_blocks, shear_offsets, block_lists, mix_weight):
        line_count = shear_blocks.shape[2]
        source = (
            jnp.arange(line_count, dtype=jnp.int32)[None, None, :, None]
            + shear_offsets[0][:, :, None, None]
            + block_lists[0][:, None]
        ) % line_count
        pipe = ("lane", "core")
        all_blocks = lax.all_gather(shear_blocks[0], pipe)
        table = lax.all_gather(source.reshape(-1), pipe).reshape(-1)
        all_mixes = lax.all_gather(mix_weight[0], pipe)
        own = lax.axis_index("lane") * 2 + lax.axis_index("half")

        parts = CHANNEL_CHUNKS
        state = turn(memory[0], parts, bands)
        state = [lax.ppermute(chunk, AXES, gather_route) for chunk in state]
        row_chunks = memory.shape[1] // ROW_TILE
        each = memory.shape[3] // bands
        out_shape = memory.shape[1:]
        for tick in range(TICKS):
            which = ((own + tick) % sections).astype(jnp.int32)[None]
            first = dense(all_blocks, table, which, 0, True)
            second = dense(all_blocks, table, which, 1, False)
            third = dense(all_blocks, table, which, 2, True)
            mixing = lax.dynamic_index_in_dim(all_mixes, which[0], keepdims=False)
            if tick < TICKS - 1:
                fields = []
                for chunk in state:
                    done = sheared(exchanged(chunk), first, second, third, None, 0)[0]
                    fields.append(exchanged(done))
                state = mixed(fields, state, mixing)
            else:
                chunk_shape = (bands, each, ROW_TILE, memory.shape[2])
                targets = [jax.ShapeDtypeStruct(chunk_shape, jnp.bfloat16)] * row_chunks
                for part, chunk in enumerate(state):
                    targets = sheared(exchanged(chunk), first, second, third, targets, part)
                out = None
                for r in range(row_chunks):
                    field = exchanged(targets[r]).reshape(-1, ROW_TILE, memory.shape[2])
                    rows = finished(field, state, mixing, r)
                    rows = lax.ppermute(rows, AXES, return_route)
                    out = placed(rows, out, r, out_shape)
        return out[None]

    return jax.shard_map(
        on_device,
        mesh=fine,
        in_specs=(
            P(("lane", "core"), ("half", "rest"), None, None),
            P(("lane", "core"), None, None, None, None, None, None),
            P(("lane", "core"), None, None),
            P(("lane", "core"), None, None, None),
            P(("lane", "core"), None, None),
        ),
        out_specs=P(("lane", "core"), ("half", "rest"), None, None),
        check_vma=False,
    )
```

```python
import jax
import jax.numpy as jnp
from jax import lax
from jax.experimental import pallas as pl
from jax.experimental.pallas import tpu as pltpu
from jax.sharding import Mesh, PartitionSpec as P

TICKS = 2
FIRST_ENDS = (5, 10, 14, 16)
LATER_ENDS = (8, 14, 16)
ROW_TILE = 16
AXES = ("lane", "core", "half", "rest")
GROUP = ("core", "rest")
VMEM = pltpu.CompilerParams(vmem_limit_bytes=58 << 20)


def cost(*arrays, products=0):
    size = sum(a.size * a.dtype.itemsize for a in arrays)
    return pl.CostEstimate(flops=2 * products, transcendentals=0, bytes_accessed=size)


def whole(shape):
    return pl.BlockSpec(shape, lambda *_: (0,) * len(shape))


def tied(value, *others):
    return lax.optimization_barrier((value, *others))[0]


def starts_of(sizes):
    return [sum(sizes[:k]) for k in range(len(sizes))]


def cut(count, ends):
    edges = [0] + [count * end // 16 for end in ends]
    return [high - low for low, high in zip(edges, edges[1:])]


def turn(memory, sizes, members):
    rows, width, channels = memory.shape
    starts = starts_of(sizes)

    def body(source, *outs):
        turned = jnp.transpose(source[...].astype(jnp.bfloat16), (2, 0, 1))
        split = turned.reshape(members, channels // members, ROW_TILE, width)
        for out, start, size in zip(outs, starts, sizes):
            out[...] = split[:, start : start + size]

    return pl.pallas_call(
        body,
        grid=(rows // ROW_TILE,),
        in_specs=[pl.BlockSpec((ROW_TILE, width, channels), lambda i: (i, 0, 0))],
        out_specs=[pl.BlockSpec((members, size, ROW_TILE, width), lambda i: (0, 0, i, 0)) for size in sizes],
        out_shape=[jax.ShapeDtypeStruct((members, size, rows, width), jnp.bfloat16) for size in sizes],
        compiler_params=VMEM,
        cost_estimate=cost(memory, memory),
        name="turn",
    )(memory)


def dense(blocks, table, which, shear, transposed, only):
    lines, outs_count, slots, wide = blocks.shape[2:6]
    size = outs_count * wide

    def body(table_ref, which_ref, source, out):
        line = pl.program_id(0)
        out[...] = jnp.zeros(out.shape, out.dtype)
        for q in range(outs_count):
            for t in range(slots):
                place = table_ref[((which_ref[0] * 3 + shear) * lines + line) * outs_count * slots + q * slots + t]
                start = pl.multiple_of(place * wide, wide)
                block = source[0, 0, 0, q, t]
                fixed = pl.ds(q * wide, wide)
                moved = pl.ds(start, wide)
                if transposed:
                    out[0, moved, fixed] += block.T
                else:
                    out[0, fixed, moved] += block

    return pl.pallas_call(
        body,
        grid_spec=pltpu.PrefetchScalarGridSpec(
            num_scalar_prefetch=2,
            grid=(lines,),
            in_specs=[
                pl.BlockSpec(
                    (1, 1, 1, outs_count, slots, wide, wide),
                    lambda i, table_ref, which_ref: (0 if only else which_ref[0], shear, i, 0, 0, 0, 0),
                )
            ],
            out_specs=pl.BlockSpec((1, size, size), lambda i, *_: (i, 0, 0)),
        ),
        out_shape=jax.ShapeDtypeStruct((lines, size, size), jnp.bfloat16),
        compiler_params=VMEM,
        cost_estimate=pl.CostEstimate(flops=0, transcendentals=0, bytes_accessed=8 * lines * size * size),
        name="dense",
    )(table, which, blocks)


def sheared(values, first, second, third, targets, start):
    members, each, rows, width = values.shape
    lines = first.shape[0]
    wide = width // lines
    per = wide // rows
    pair = 2 if each % 2 == 0 and start % 2 == 0 else 1
    count = len(targets)

    def body(source, first_ref, second_ref, third_ref, *refs):
        outs, (one, two) = refs[-2 - count : -2], refs[-2:]
        for ch in range(pair):
            for i in range(lines):
                lhs = source[per * i : per * (i + 1), ch].reshape(wide, width)
                got = jnp.dot(lhs, first_ref[i], preferred_element_type=jnp.float32).astype(jnp.bfloat16)
                for j in range(lines):
                    one[j, i * wide : (i + 1) * wide, ch * wide : (ch + 1) * wide] = got[:, j * wide : (j + 1) * wide]
        for j in range(lines):
            got = jnp.dot(second_ref[j], one[j], preferred_element_type=jnp.float32).astype(jnp.bfloat16)
            for ch in range(pair):
                two[ch, :, j * wide : (j + 1) * wide] = got[:, ch * wide : (ch + 1) * wide]
        for ch in range(pair):
            for i in range(lines):
                lhs = two[ch, i * wide : (i + 1) * wide]
                got = jnp.dot(lhs, third_ref[i], preferred_element_type=jnp.float32).astype(jnp.bfloat16)
                split = got.reshape(per, count, rows // count, width)
                for r in range(count):
                    outs[r][per * i : per * (i + 1), ch] = split[:, r]

    steps, base = each // pair, start // pair
    given = targets if start else []
    out_rows = rows // count
    return pl.pallas_call(
        body,
        grid=(steps,),
        in_specs=[pl.BlockSpec((members, pair, rows, width), lambda c: (0, c, 0, 0))]
        + [whole(first.shape)] * 3
        + [pl.BlockSpec(memory_space=pl.ANY)] * len(given),
        out_specs=[pl.BlockSpec((members, pair, out_rows, width), lambda c: (0, base + c, 0, 0))] * count,
        out_shape=[jax.ShapeDtypeStruct(target.shape, jnp.bfloat16) for target in targets],
        scratch_shapes=[
            pltpu.VMEM((lines, width, pair * wide), jnp.bfloat16),
            pltpu.VMEM((pair, width, width), jnp.bfloat16),
        ],
        input_output_aliases={4 + r: r for r in range(len(given))},
        compiler_params=VMEM,
        cost_estimate=cost(values, values, first, first, first, products=6 * values.size * width),
        name="sheared",
    )(values, first, second, third, *given)


def joined(refs, members):
    return jnp.concatenate([ref[j] for j in range(members) for ref in refs], axis=0)


def mixed(fields, state, mixing, sizes):
    members, _, rows, width = fields[0].shape
    starts = starts_of(sizes)
    channels = mixing.shape[0]
    ends = len(fields), len(fields) + len(state)

    def body(*refs):
        mix = refs[ends[1]][...]
        outs = refs[ends[1] + 1 :]
        turned = jnp.swapaxes(joined(refs[: ends[0]], members), 0, 1)
        got = [
            lax.dot_general(mix, turned[l], (((0,), (0,)), ((), ())), preferred_element_type=jnp.float32)
            for l in range(ROW_TILE)
        ]
        back = jnp.swapaxes(jnp.stack([g.astype(jnp.bfloat16) for g in got], 0), 0, 1)
        total = joined(refs[ends[0] : ends[1]], members).astype(jnp.float32) + back.astype(jnp.float32)
        split = total.astype(jnp.bfloat16).reshape(members, channels // members, ROW_TILE, width)
        for out, start, size in zip(outs, starts, sizes):
            out[...] = split[:, start : start + size]

    def block(size):
        return pl.BlockSpec((members, size, ROW_TILE, width), lambda i: (0, 0, i, 0))

    return pl.pallas_call(
        body,
        grid=(rows // ROW_TILE,),
        in_specs=[block(a.shape[1]) for a in (*fields, *state)] + [whole((channels, channels))],
        out_specs=[block(size) for size in sizes],
        out_shape=[jax.ShapeDtypeStruct((members, size, rows, width), jnp.bfloat16) for size in sizes],
        compiler_params=VMEM,
        cost_estimate=cost(*fields, *fields, *fields, *state, *state),
        name="mixed",
    )(*fields, *state, mixing)


def finished(field, state, mixing, row_chunk):
    channels, rows, width = field.shape
    parts = len(state)
    members = state[0].shape[0]
    piece = min(width, 128)

    def body(*refs):
        mix = refs[1 + parts][...]
        out = refs[2 + parts]
        turned = jnp.swapaxes(refs[0][...], 0, 1)
        old = jnp.swapaxes(joined(refs[1 : 1 + parts], members), 0, 1)
        for l in range(rows):
            got = lax.dot_general(mix, turned[l], (((0,), (0,)), ((), ())), preferred_element_type=jnp.float32)
            out[l] = (got + old[l].astype(jnp.float32)).astype(jnp.bfloat16).T

    return pl.pallas_call(
        body,
        grid=(width // piece,),
        in_specs=[pl.BlockSpec((channels, rows, piece), lambda i: (0, 0, i))]
        + [pl.BlockSpec((members, old.shape[1], rows, piece), lambda i: (0, 0, row_chunk, i)) for old in state]
        + [whole((channels, channels))],
        out_specs=pl.BlockSpec((rows, piece, channels), lambda i: (0, i, 0)),
        out_shape=jax.ShapeDtypeStruct((rows, width, channels), jnp.bfloat16),
        compiler_params=VMEM,
        cost_estimate=cost(*[field] * 8),
        name="finished",
    )(field, *state, mixing)


def placed(rows_in, target, row_chunk, shape):
    rows, width, channels = rows_in.shape
    piece = min(width, 128)

    def body(source, *refs):
        refs[-1][...] = source[...].astype(jnp.float32)

    given = [] if target is None else [target]
    return pl.pallas_call(
        body,
        grid=(width // piece,),
        in_specs=[pl.BlockSpec((rows, piece, channels), lambda i: (0, i, 0))]
        + [pl.BlockSpec(memory_space=pl.ANY)] * len(given),
        out_specs=pl.BlockSpec((rows, piece, channels), lambda i: (row_chunk, i, 0)),
        out_shape=jax.ShapeDtypeStruct(shape, jnp.float32),
        input_output_aliases={1: 0} if given else {},
        compiler_params=VMEM,
        cost_estimate=cost(*[rows_in] * 4),
        name="placed",
    )(rows_in, *given)


def exchanged(values):
    return lax.all_to_all(values, GROUP, split_axis=0, concat_axis=0, tiled=True)


def solution(mesh):
    sections = mesh.shape["pipe"]
    bands = mesh.shape["band"]
    lanes, rest = sections // 2, bands // 2
    fine = Mesh(mesh.devices.reshape(lanes, 2, 2, rest), AXES)

    def flat(pipe, half, place):
        return (pipe * 2 + half) * rest + place

    gather_route = []
    return_route = []
    for lane in range(lanes):
        for core in range(2):
            for half in range(2):
                for place in range(rest):
                    here = flat(lane * 2 + core, half, place)
                    gather_route.append((here, flat(lane * 2 + half, core, place)))
                    owner = (lane * 2 + half + TICKS) % sections
                    return_route.append((here, flat(owner, core, place)))

    def on_device(memory, shear_blocks, shear_offsets, block_lists, mix_weight):
        line_count = shear_blocks.shape[2]
        source = (
            jnp.arange(line_count, dtype=jnp.int32)[None, None, :, None]
            + shear_offsets[0][:, :, None, None]
            + block_lists[0][:, None]
        ) % line_count
        pipe = ("lane", "core")
        core, half = lax.axis_index("core"), lax.axis_index("half")
        own = lax.axis_index("lane") * 2 + half
        other_blocks = lax.ppermute(shear_blocks[0], "core", [(0, 1), (1, 0)])
        blocks = jnp.where(core == half, shear_blocks[0], other_blocks)[None]
        table = lax.all_gather(source.reshape(-1), pipe).reshape(-1)
        all_blocks = lax.all_gather(shear_blocks[0], pipe)
        all_mixes = lax.all_gather(mix_weight[0], pipe)

        members, (_, height, width, channels) = bands, memory.shape
        each = channels // members
        row_chunks = height // ROW_TILE
        out_shape = memory.shape[1:]

        def room(rows):
            return jax.ShapeDtypeStruct((members, each, rows, width), jnp.bfloat16)

        def matrices(tick, held):
            which = ((own + tick) % sections).astype(jnp.int32)[None]
            only = tick == 0
            mixing = lax.dynamic_index_in_dim(all_mixes, which[0], keepdims=False)
            return [dense(held, table, which, k, k != 1, only) for k in range(3)], mixing

        def section_shears(sent, weights, targets, route):
            starts = starts_of([chunk.shape[1] for chunk in sent])
            here, full = [], []
            for k, chunk in enumerate(sent):
                if route:
                    chunk = lax.ppermute(tied(chunk, here[-1]) if k else chunk, AXES, gather_route)
                here.append(chunk)
                arrived = exchanged(tied(chunk, *targets) if k > 1 else chunk)
                if k:
                    targets = sheared(full[-1], *weights, targets, starts[k - 1])
                    arrived = tied(arrived, *targets)
                full.append(arrived)
            return here, sheared(full[-1], *weights, targets, starts[-1])

        sent = turn(memory[0], cut(each, FIRST_ENDS), members)
        for tick in range(TICKS):
            last = tick == TICKS - 1
            weights, mixing = matrices(tick, all_blocks if tick else blocks)
            targets = [room(ROW_TILE)] * row_chunks if last else [room(height)]
            state, targets = section_shears(sent, weights, targets, tick == 0)
            if not last:
                sent = mixed([exchanged(targets[0])], state, mixing, cut(each, LATER_ENDS))
        out, rows = None, None
        moved = []
        for r in range(row_chunks):
            waits = ([rows] if r else []) + (moved[r - 2 : r - 1] if r > 1 else [])
            field = exchanged(tied(targets[r], *waits) if waits else targets[r])
            if r > 1 and r == row_chunks - 1:
                field = tied(field, moved[-1])
            rows = finished(field.reshape(-1, ROW_TILE, width), state, mixing, r)
            moved.append(lax.ppermute(rows, AXES, return_route))
        for r in range(row_chunks):
            out = placed(moved[r], out, r, out_shape)
        return out[None]

    return jax.shard_map(
        on_device,
        mesh=fine,
        in_specs=(
            P(("lane", "core"), ("half", "rest"), None, None),
            P(("lane", "core"), None, None, None, None, None, None),
            P(("lane", "core"), None, None),
            P(("lane", "core"), None, None, None),
            P(("lane", "core"), None, None),
        ),
        out_specs=P(("lane", "core"), ("half", "rest"), None, None),
        check_vma=False,
    )
```

```python
import jax
import jax.numpy as jnp
from jax import lax
from jax.experimental import pallas as pl
from jax.experimental.pallas import tpu as pltpu
from jax.sharding import Mesh, PartitionSpec as P

TICKS = 2
ENDS = (4, 8, 12, 16)
ROW_TILE = 16
AXES = ("lane", "core", "half", "rest")
GROUP = ("core", "rest")
VMEM = pltpu.CompilerParams(vmem_limit_bytes=58 << 20)


def cost(*arrays, products=0):
    size = sum(a.size * a.dtype.itemsize for a in arrays)
    return pl.CostEstimate(flops=2 * products, transcendentals=0, bytes_accessed=size)


def whole(shape):
    return pl.BlockSpec(shape, lambda *_: (0,) * len(shape))


def tied(value, *others):
    return lax.optimization_barrier((value, *others))[0]


def starts_of(sizes):
    return [sum(sizes[:k]) for k in range(len(sizes))]


def cut(count, ends):
    edges = [0] + [count * end // 16 for end in ends]
    return [high - low for low, high in zip(edges, edges[1:])]


def spread(memory, sizes, members, band):
    rows, width, channels = memory.shape
    each = channels // members
    starts = starts_of(sizes)

    def body(band_ref, source, *refs):
        outs, kept = refs[:-1], refs[-1]
        turned = jnp.transpose(source[...].astype(jnp.bfloat16), (2, 0, 1))
        kept[...] = turned.reshape(members, each, ROW_TILE, width)
        for c, (start, size) in enumerate(zip(starts, sizes)):
            for k in range(members):
                outs[c * members + k][...] = kept[band_ref[0] ^ k, start : start + size]

    pieces = [size for size in sizes for _ in range(members)]
    outs = pl.pallas_call(
        body,
        grid_spec=pltpu.PrefetchScalarGridSpec(
            num_scalar_prefetch=1,
            grid=(rows // ROW_TILE,),
            in_specs=[pl.BlockSpec((ROW_TILE, width, channels), lambda i, _: (i, 0, 0))],
            out_specs=[pl.BlockSpec((size, ROW_TILE, width), lambda i, _: (0, i, 0)) for size in pieces],
            scratch_shapes=[pltpu.VMEM((members, each, ROW_TILE, width), jnp.bfloat16)],
        ),
        out_shape=[jax.ShapeDtypeStruct((size, rows, width), jnp.bfloat16) for size in pieces],
        compiler_params=VMEM,
        cost_estimate=cost(memory, memory),
        name="spread",
    )(band, memory)
    return [outs[c * members : (c + 1) * members] for c in range(len(sizes))]


def packed(table, mixing):
    wide = mixing.shape[-1]
    numbers = table.reshape(-1).astype(jnp.bfloat16)
    short = -(-numbers.size // wide)
    short += -short % 16
    numbers = jnp.pad(numbers, (0, short * wide - numbers.size)).reshape(short, wide)
    return jnp.concatenate([mixing, numbers], axis=0)


def dense(blocks, table, which, shear, transposed):
    lines, outs_count, slots, wide = blocks.shape[2:6]
    size = outs_count * wide

    def body(table_ref, _, source, out):
        line = pl.program_id(0)
        out[...] = jnp.zeros(out.shape, out.dtype)
        for q in range(outs_count):
            for t in range(slots):
                place = table_ref[((shear * lines + line) * outs_count + q) * slots + t]
                start = pl.multiple_of(place * wide, wide)
                block = source[0, 0, 0, q, t]
                fixed = pl.ds(q * wide, wide)
                moved = pl.ds(start, wide)
                if transposed:
                    out[0, moved, fixed] += block.T
                else:
                    out[0, fixed, moved] += block

    return pl.pallas_call(
        body,
        grid_spec=pltpu.PrefetchScalarGridSpec(
            num_scalar_prefetch=2,
            grid=(lines,),
            in_specs=[
                pl.BlockSpec(
                    (1, 1, 1, outs_count, slots, wide, wide),
                    lambda i, _, which_ref: (which_ref[0], shear, i, 0, 0, 0, 0),
                )
            ],
            out_specs=pl.BlockSpec((1, size, size), lambda i, *_: (i, 0, 0)),
        ),
        out_shape=jax.ShapeDtypeStruct((lines, size, size), jnp.bfloat16),
        compiler_params=VMEM,
        cost_estimate=pl.CostEstimate(flops=0, transcendentals=0, bytes_accessed=8 * lines * size * size),
        name="dense",
    )(table, which, blocks)


def relayed(values, member, first, second, row_chunks):
    members = len(values)
    each, rows, width = values[0].shape
    lines = first[0].shape[0]
    wide = width // lines
    per = wide // rows
    pair = 2 if each % 2 == 0 else 1
    height = rows // row_chunks

    def body(member_ref, *refs):
        pieces, mats = refs[:members], refs[members : members + 6]
        outs, (source, kept, one, two) = refs[members + 6 : members + 6 + row_chunks], refs[members + 6 + row_chunks :]
        for k in range(members):
            source[member_ref[0] ^ k] = pieces[k][...]

        def shears(load, k, slots):
            for s in range(len(slots)):
                for i in range(lines):
                    got = jnp.dot(load(s, i), mats[3 * k][i], preferred_element_type=jnp.float32).astype(jnp.bfloat16)
                    for j in range(lines):
                        one[j, i * wide : (i + 1) * wide, s * wide : (s + 1) * wide] = got[:, j * wide : (j + 1) * wide]
            span = len(slots) * wide
            for j in range(lines):
                got = jnp.dot(mats[3 * k + 1][j], one[j, :, :span], preferred_element_type=jnp.float32)
                got = got.astype(jnp.bfloat16)
                for s in range(len(slots)):
                    two[s, :, j * wide : (j + 1) * wide] = got[:, s * wide : (s + 1) * wide]
            for s, (term, ch) in enumerate(slots):
                for i in range(lines):
                    lhs = two[s, i * wide : (i + 1) * wide]
                    got = jnp.dot(lhs, mats[3 * k + 2][i], preferred_element_type=jnp.float32).astype(jnp.bfloat16)
                    if term == 0:
                        kept[ch, i * wide : (i + 1) * wide] = got
                    split = got.reshape(per, row_chunks, height, width)
                    for r in range(row_chunks):
                        outs[r][per * i : per * (i + 1), term, ch] = split[:, r]

        def given(ch, i):
            return source[per * i : per * (i + 1), ch].reshape(wide, width)

        def held(s, i):
            if s < pair:
                return given(s, i)
            return kept[s - pair, i * wide : (i + 1) * wide]

        shears(given, 0, [(0, ch) for ch in range(pair)])
        shears(held, 1, [(term, ch) for term in (1, 2) for ch in range(pair)])

    mat = pl.BlockSpec(first[0].shape, lambda c, _: (0, 0, 0), pipeline_mode=pl.Buffered(1))
    return pl.pallas_call(
        body,
        grid_spec=pltpu.PrefetchScalarGridSpec(
            num_scalar_prefetch=1,
            grid=(each // pair,),
            in_specs=[pl.BlockSpec((pair, rows, width), lambda c, _: (c, 0, 0))] * members + [mat] * 6,
            out_specs=[pl.BlockSpec((members, 3, pair, height, width), lambda c, _: (0, 0, c, 0, 0))] * row_chunks,
            scratch_shapes=[
                pltpu.VMEM((members, pair, rows, width), jnp.bfloat16),
                pltpu.VMEM((pair, width, width), jnp.bfloat16),
                pltpu.VMEM((lines, width, 2 * pair * wide), jnp.bfloat16),
                pltpu.VMEM((2 * pair, width, width), jnp.bfloat16),
            ],
        ),
        out_shape=[jax.ShapeDtypeStruct((members, 3, each, height, width), jnp.bfloat16)] * row_chunks,
        compiler_params=VMEM,
        cost_estimate=cost(*values * 4, *first, *second, products=18 * members * values[0].size * width),
        name="relayed",
    )(member, *values, *first, *second)


def finished(terms, last, mixes, row_chunk):
    members, _, _, rows, width = last.shape
    channels = mixes[0].shape[0]
    piece = min(width, 128)
    count = len(terms) + 1

    def body(*refs):
        fields, one, two, out = refs[:count], refs[count][...], refs[count + 1][...], refs[count + 2]

        def by_row(pick):
            parts = [pick(j, k) for j in range(members) for k in range(count)]
            return jnp.swapaxes(jnp.concatenate(parts, axis=0), 0, 1)

        p, q, r = [by_row(lambda j, k: fields[k][j, term]) for term in range(3)]
        over_rows = (((0,), (0,)), ((), ()))
        for l in range(rows):
            both = jnp.concatenate([p[l], r[l]], axis=1)
            got = lax.dot_general(one, both, over_rows, preferred_element_type=jnp.float32)
            more = (q[l].astype(jnp.float32) + got[:, piece:]).astype(jnp.bfloat16)
            total = got[:, :piece] + lax.dot_general(two, more, over_rows, preferred_element_type=jnp.float32)
            out[l] = total.astype(jnp.bfloat16).T

    def term_block(a, at):
        return pl.BlockSpec((members, 3, a.shape[2], rows, piece), lambda i: (0, 0, 0, at, i))

    return pl.pallas_call(
        body,
        grid=(width // piece,),
        in_specs=[term_block(a, row_chunk) for a in terms]
        + [term_block(last, 0)]
        + [whole((channels, channels))] * 2,
        out_specs=pl.BlockSpec((rows, piece, channels), lambda i: (0, i, 0)),
        out_shape=jax.ShapeDtypeStruct((rows, width, channels), jnp.bfloat16),
        compiler_params=VMEM,
        cost_estimate=cost(last, last, last),
        name="finished",
    )(*terms, last, *mixes)


def placed(rows_in, old, target, row_chunk, shape):
    rows, width, channels = rows_in.shape
    piece = min(width, 128)

    def body(source, before, *refs):
        refs[-1][...] = before[...].astype(jnp.float32) + source[...].astype(jnp.float32)

    given = [] if target is None else [target]
    block = pl.BlockSpec((rows, piece, channels), lambda i: (0, i, 0))
    return pl.pallas_call(
        body,
        grid=(width // piece,),
        in_specs=[block, block] + [pl.BlockSpec(memory_space=pl.ANY)] * len(given),
        out_specs=pl.BlockSpec((rows, piece, channels), lambda i: (row_chunk, i, 0)),
        out_shape=jax.ShapeDtypeStruct(shape, jnp.float32),
        input_output_aliases={2: 0} if given else {},
        compiler_params=VMEM,
        cost_estimate=cost(*[rows_in] * 5),
        name="placed",
    )(rows_in, old, *given)


def exchanged(values):
    return lax.all_to_all(values, GROUP, split_axis=0, concat_axis=0, tiled=True)


def solution(mesh):
    sections = mesh.shape["pipe"]
    bands = mesh.shape["band"]
    lanes, rest = sections // 2, bands // 2
    fine = Mesh(mesh.devices.reshape(lanes, 2, 2, rest), AXES)

    def flat(pipe, half, place):
        return (pipe * 2 + half) * rest + place

    places = [(pipe, band) for pipe in range(sections) for band in range(bands)]

    def at(pipe, band):
        return pipe * bands + band

    def hosts(section, member):
        return at(section // 2 * 2 + member // rest, section % 2 * rest + member % rest)

    spread_routes = [[(at(p, b), hosts(p, b ^ k)) for p, b in places] for k in range(bands)]
    shift_route = [(at(p, b), at((p + TICKS) % sections, b)) for p, b in places]
    return_route = [(hosts(p, b), at((p + TICKS) % sections, b)) for p, b in places]

    def on_device(memory, shear_blocks, shear_offsets, block_lists, mix_weight):
        line_count = shear_blocks.shape[2]
        source = (
            jnp.arange(line_count, dtype=jnp.int32)[None, None, :, None]
            + shear_offsets[0][:, :, None, None]
            + block_lists[0][:, None]
        ) % line_count
        pipe = ("lane", "core")
        own = lax.axis_index("lane") * 2 + lax.axis_index("half")
        all_blocks = lax.all_gather(shear_blocks[0], pipe)
        packs = lax.all_gather(packed(source, mix_weight[0]), pipe)

        members, (_, height, width, channels) = bands, memory.shape
        row_chunks = height // ROW_TILE
        out_shape = memory.shape[1:]
        mix_rows = mix_weight.shape[1]
        weights, mixes = [], []
        for tick in range(TICKS):
            which = ((own + tick) % sections).astype(jnp.int32)[None]
            tail = lax.dynamic_index_in_dim(packs, which[0], keepdims=False)
            table = tail[mix_rows:].reshape(-1)[: source.size].astype(jnp.int32)
            weights.append([dense(all_blocks, table, which, k, k != 1) for k in range(3)])
            mixes.append(tail[:mix_rows])

        band = (lax.axis_index("half") * rest + lax.axis_index("rest")).astype(jnp.int32)[None]
        member = (lax.axis_index("core") * rest + lax.axis_index("rest")).astype(jnp.int32)[None]
        sent = spread(memory[0], cut(channels // members, ENDS), members, band)
        last = len(sent) - 1

        def shifted(r, *waits):
            rows = memory[0, r * ROW_TILE : (r + 1) * ROW_TILE].astype(jnp.bfloat16)
            return lax.ppermute(tied(rows, *waits), AXES, shift_route)

        def delivered(k, *waits):
            pieces = sent[k]
            if waits:
                pieces = lax.optimization_barrier((*pieces, *waits))[:members]
            return [lax.ppermute(piece, AXES, route) for piece, route in zip(pieces, spread_routes)]

        def later(values, *waits):
            return lax.optimization_barrier((*values, *waits))[: len(values)]

        full = delivered(0, packs)
        terms, olds = [], []
        for k in range(last):
            (solved,) = relayed(full, member, *weights, 1)
            waits = [solved] if k else []
            if terms:
                terms[-1], solved = later([terms[-1], solved])
            full = delivered(k + 1, *full, *waits)
            if k:
                olds += [shifted(r, *olds[-1:], *waits) for r in range(len(olds), -(-row_chunks * k // last))]
            (solved,) = later([solved], *full, *olds)
            terms.append(exchanged(solved.reshape(members, -1, height, width)).reshape(solved.shape))
        solved = relayed(full, member, *weights, row_chunks)
        olds += [shifted(r, *olds[-1:], solved[0]) for r in range(len(olds), row_chunks)]
        terms[-1], *solved = later([terms[-1], *solved])
        solved = later(solved, *olds)

        out, rows = None, None
        moved = []
        for r in range(row_chunks):
            waits = ([rows] if r else []) + (moved[r - 2 : r - 1] if r > 1 else [])
            field = solved[r].reshape(members, -1, ROW_TILE, width)
            field = exchanged(tied(field, *waits) if waits else field)
            if r > 1 and r == row_chunks - 1:
                field = tied(field, moved[-1])
            rows = finished(terms, field.reshape(solved[r].shape), mixes, r)
            moved.append(lax.ppermute(rows, AXES, return_route))
        for r in range(row_chunks):
            out = placed(moved[r], olds[r], out, r, out_shape)
        return out[None]

    return jax.shard_map(
        on_device,
        mesh=fine,
        in_specs=(
            P(("lane", "core"), ("half", "rest"), None, None),
            P(("lane", "core"), None, None, None, None, None, None),
            P(("lane", "core"), None, None),
            P(("lane", "core"), None, None, None),
            P(("lane", "core"), None, None),
        ),
        out_specs=P(("lane", "core"), ("half", "rest"), None, None),
        check_vma=False,
    )
```

```python
import jax
import jax.numpy as jnp
from jax import lax
from jax.experimental import pallas as pl
from jax.experimental.pallas import tpu as pltpu
from jax.sharding import Mesh, PartitionSpec as P

TICKS = 2
ENDS = (4, 8, 12, 16)
ROW_TILE = 16
PIECE = 512
AXES = ("lane", "core", "half", "rest")
GROUP = ("core", "rest")
VMEM = pltpu.CompilerParams(vmem_limit_bytes=58 << 20)


def cost(*arrays, products=0):
    size = sum(a.size * a.dtype.itemsize for a in arrays)
    return pl.CostEstimate(flops=2 * products, transcendentals=0, bytes_accessed=size)


def whole(shape):
    return pl.BlockSpec(shape, lambda *_: (0,) * len(shape))


def tied(value, *others):
    return lax.optimization_barrier((value, *others))[0]


def starts_of(sizes):
    return [sum(sizes[:k]) for k in range(len(sizes))]


def cut(count, ends):
    edges = [0] + [count * end // 16 for end in ends]
    return [high - low for low, high in zip(edges, edges[1:])]


def spread(memory, sizes, members, band):
    rows, width, channels = memory.shape
    each = channels // members
    starts = starts_of(sizes)

    def body(band_ref, source, *refs):
        outs, kept = refs[:-1], refs[-1]
        turned = jnp.transpose(source[...].astype(jnp.bfloat16), (2, 0, 1))
        kept[...] = turned.reshape(members, each, ROW_TILE, width)
        for c, (start, size) in enumerate(zip(starts, sizes)):
            for k in range(members):
                outs[c * members + k][...] = kept[band_ref[0] ^ k, start : start + size]

    pieces = [size for size in sizes for _ in range(members)]
    outs = pl.pallas_call(
        body,
        grid_spec=pltpu.PrefetchScalarGridSpec(
            num_scalar_prefetch=1,
            grid=(rows // ROW_TILE,),
            in_specs=[pl.BlockSpec((ROW_TILE, width, channels), lambda i, _: (i, 0, 0))],
            out_specs=[pl.BlockSpec((size, ROW_TILE, width), lambda i, _: (0, i, 0)) for size in pieces],
            scratch_shapes=[pltpu.VMEM((members, each, ROW_TILE, width), jnp.bfloat16)],
        ),
        out_shape=[jax.ShapeDtypeStruct((size, rows, width), jnp.bfloat16) for size in pieces],
        compiler_params=VMEM,
        cost_estimate=cost(memory, memory),
        name="spread",
    )(band, memory)
    return [outs[c * members : (c + 1) * members] for c in range(len(sizes))]


def packed(table, mixing):
    wide = mixing.shape[-1]
    numbers = table.reshape(-1).astype(jnp.bfloat16)
    short = -(-numbers.size // wide)
    short += -short % 16
    numbers = jnp.pad(numbers, (0, short * wide - numbers.size)).reshape(short, wide)
    return jnp.concatenate([mixing, numbers], axis=0)


def dense(blocks, table, which, shear, transposed):
    lines, outs_count, slots, wide = blocks.shape[2:6]
    size = outs_count * wide

    def body(table_ref, _, source, out):
        line = pl.program_id(0)
        out[...] = jnp.zeros(out.shape, out.dtype)
        for q in range(outs_count):
            for t in range(slots):
                place = table_ref[((shear * lines + line) * outs_count + q) * slots + t]
                start = pl.multiple_of(place * wide, wide)
                block = source[0, 0, 0, q, t]
                fixed = pl.ds(q * wide, wide)
                moved = pl.ds(start, wide)
                if transposed:
                    out[0, moved, fixed] += block.T
                else:
                    out[0, fixed, moved] += block

    return pl.pallas_call(
        body,
        grid_spec=pltpu.PrefetchScalarGridSpec(
            num_scalar_prefetch=2,
            grid=(lines,),
            in_specs=[
                pl.BlockSpec(
                    (1, 1, 1, outs_count, slots, wide, wide),
                    lambda i, _, which_ref: (which_ref[0], shear, i, 0, 0, 0, 0),
                )
            ],
            out_specs=pl.BlockSpec((1, size, size), lambda i, *_: (i, 0, 0)),
        ),
        out_shape=jax.ShapeDtypeStruct((lines, size, size), jnp.bfloat16),
        compiler_params=VMEM,
        cost_estimate=pl.CostEstimate(flops=0, transcendentals=0, bytes_accessed=8 * lines * size * size),
        name="dense",
    )(table, which, blocks)


def relayed(values, member, first, second, targets, start):
    row_chunks = len(targets)
    members = len(values)
    each, rows, width = values[0].shape
    lines = first[0].shape[0]
    wide = width // lines
    per = wide // rows
    pair = 2 if each % 2 == 0 and start % 2 == 0 else 1
    base = start // pair
    given = targets if start else []
    height = rows // row_chunks

    def body(member_ref, *refs):
        pieces, mats = refs[:members], refs[members : members + 6]
        outs, (source, kept, one, two) = refs[-4 - row_chunks : -4], refs[-4:]
        for k in range(members):
            source[member_ref[0] ^ k] = pieces[k][...]

        def shears(load, k, slots):
            for s in range(len(slots)):
                for i in range(lines):
                    got = jnp.dot(load(s, i), mats[3 * k][i], preferred_element_type=jnp.float32).astype(jnp.bfloat16)
                    for j in range(lines):
                        one[j, i * wide : (i + 1) * wide, s * wide : (s + 1) * wide] = got[:, j * wide : (j + 1) * wide]
            span = len(slots) * wide
            for j in range(lines):
                got = jnp.dot(mats[3 * k + 1][j], one[j, :, :span], preferred_element_type=jnp.float32)
                got = got.astype(jnp.bfloat16)
                for s in range(len(slots)):
                    two[s, :, j * wide : (j + 1) * wide] = got[:, s * wide : (s + 1) * wide]
            for s, (term, ch) in enumerate(slots):
                for i in range(lines):
                    lhs = two[s, i * wide : (i + 1) * wide]
                    got = jnp.dot(lhs, mats[3 * k + 2][i], preferred_element_type=jnp.float32).astype(jnp.bfloat16)
                    if term == 0:
                        kept[ch, i * wide : (i + 1) * wide] = got
                    split = got.reshape(per, row_chunks, height, width)
                    for r in range(row_chunks):
                        outs[r][per * i : per * (i + 1), term, ch] = split[:, r]

        def fresh(ch, i):
            return source[per * i : per * (i + 1), ch].reshape(wide, width)

        def held(s, i):
            if s < pair:
                return fresh(s, i)
            return kept[s - pair, i * wide : (i + 1) * wide]

        shears(fresh, 0, [(0, ch) for ch in range(pair)])
        shears(held, 1, [(term, ch) for term in (1, 2) for ch in range(pair)])

    mat = pl.BlockSpec(first[0].shape, lambda c, _: (0, 0, 0), pipeline_mode=pl.Buffered(1))
    return pl.pallas_call(
        body,
        grid_spec=pltpu.PrefetchScalarGridSpec(
            num_scalar_prefetch=1,
            grid=(each // pair,),
            in_specs=[pl.BlockSpec((pair, rows, width), lambda c, _: (c, 0, 0))] * members
            + [mat] * 6
            + [pl.BlockSpec(memory_space=pl.ANY)] * len(given),
            out_specs=[pl.BlockSpec((members, 3, pair, height, width), lambda c, _: (0, 0, base + c, 0, 0))] * row_chunks,
            scratch_shapes=[
                pltpu.VMEM((members, pair, rows, width), jnp.bfloat16),
                pltpu.VMEM((pair, width, width), jnp.bfloat16),
                pltpu.VMEM((lines, width, 2 * pair * wide), jnp.bfloat16),
                pltpu.VMEM((2 * pair, width, width), jnp.bfloat16),
            ],
        ),
        out_shape=[jax.ShapeDtypeStruct(target.shape, jnp.bfloat16) for target in targets],
        input_output_aliases={1 + members + 6 + r: r for r in range(len(given))},
        compiler_params=VMEM,
        cost_estimate=cost(*values * 4, *first, *second, products=18 * members * values[0].size * width),
        name="relayed",
    )(member, *values, *first, *second, *given)


def finished(terms, last, mixes, row_chunk):
    members, _, _, rows, width = last.shape
    channels = mixes[0].shape[0]
    piece = min(width, PIECE)
    count = len(terms) + 1

    def body(*refs):
        fields, one, two, out = refs[:count], refs[count][...], refs[count + 1][...], refs[count + 2]

        def by_row(pick):
            parts = [pick(j, k) for j in range(members) for k in range(count)]
            return jnp.swapaxes(jnp.concatenate(parts, axis=0), 0, 1)

        p, q, r = [by_row(lambda j, k: fields[k][j, term]) for term in range(3)]
        over_rows = (((0,), (0,)), ((), ()))
        for l in range(rows):
            both = jnp.concatenate([p[l], r[l]], axis=1)
            got = lax.dot_general(one, both, over_rows, preferred_element_type=jnp.float32)
            more = (q[l].astype(jnp.float32) + got[:, piece:]).astype(jnp.bfloat16)
            total = got[:, :piece] + lax.dot_general(two, more, over_rows, preferred_element_type=jnp.float32)
            out[l] = total.astype(jnp.bfloat16).T

    def term_block(a, at):
        return pl.BlockSpec((members, 3, a.shape[2], rows, piece), lambda i: (0, 0, 0, at, i))

    return pl.pallas_call(
        body,
        grid=(width // piece,),
        in_specs=[term_block(a, row_chunk) for a in terms]
        + [term_block(last, 0)]
        + [whole((channels, channels))] * 2,
        out_specs=pl.BlockSpec((rows, piece, channels), lambda i: (0, i, 0)),
        out_shape=jax.ShapeDtypeStruct((rows, width, channels), jnp.bfloat16),
        compiler_params=VMEM,
        cost_estimate=cost(last, last, last),
        name="finished",
    )(*terms, last, *mixes)


def placed(rows_in, old, target, row_chunk, shape):
    rows, width, channels = rows_in.shape
    piece = min(width, 128)

    def body(source, before, *refs):
        refs[-1][...] = before[...].astype(jnp.float32) + source[...].astype(jnp.float32)

    given = [] if target is None else [target]
    block = pl.BlockSpec((rows, piece, channels), lambda i: (0, i, 0))
    return pl.pallas_call(
        body,
        grid=(width // piece,),
        in_specs=[block, pl.BlockSpec((rows, piece, channels), lambda i: (row_chunk, i, 0))] + [pl.BlockSpec(memory_space=pl.ANY)] * len(given),
        out_specs=pl.BlockSpec((rows, piece, channels), lambda i: (row_chunk, i, 0)),
        out_shape=jax.ShapeDtypeStruct(shape, jnp.float32),
        input_output_aliases={2: 0} if given else {},
        compiler_params=VMEM,
        cost_estimate=cost(*[rows_in] * 5),
        name="placed",
    )(rows_in, old, *given)


def exchanged(values):
    return lax.all_to_all(values, GROUP, split_axis=0, concat_axis=0, tiled=True)


def solution(mesh):
    sections = mesh.shape["pipe"]
    bands = mesh.shape["band"]
    lanes, rest = sections // 2, bands // 2
    fine = Mesh(mesh.devices.reshape(lanes, 2, 2, rest), AXES)

    def flat(pipe, half, place):
        return (pipe * 2 + half) * rest + place

    places = [(pipe, band) for pipe in range(sections) for band in range(bands)]

    def at(pipe, band):
        return pipe * bands + band

    def hosts(section, member):
        return at(section // 2 * 2 + member // rest, section % 2 * rest + member % rest)

    spread_routes = [[(at(p, b), hosts(p, b ^ k)) for p, b in places] for k in range(bands)]
    shift_route = [(at(p, b), at((p + TICKS) % sections, b)) for p, b in places]
    return_route = [(hosts(p, b), at((p + TICKS) % sections, b)) for p, b in places]

    def on_device(memory, shear_blocks, shear_offsets, block_lists, mix_weight):
        line_count = shear_blocks.shape[2]
        source = (
            jnp.arange(line_count, dtype=jnp.int32)[None, None, :, None]
            + shear_offsets[0][:, :, None, None]
            + block_lists[0][:, None]
        ) % line_count
        pipe = ("lane", "core")
        own = lax.axis_index("lane") * 2 + lax.axis_index("half")
        all_blocks = lax.all_gather(shear_blocks[0], pipe)
        packs = lax.all_gather(packed(source, mix_weight[0]), pipe)

        members, (_, height, width, channels) = bands, memory.shape
        row_chunks = height // ROW_TILE
        out_shape = memory.shape[1:]
        mix_rows = mix_weight.shape[1]
        weights, mixes = [], []
        for tick in range(TICKS):
            which = ((own + tick) % sections).astype(jnp.int32)[None]
            tail = lax.dynamic_index_in_dim(packs, which[0], keepdims=False)
            table = tail[mix_rows:].reshape(-1)[: source.size].astype(jnp.int32)
            weights.append([dense(all_blocks, table, which, k, k != 1) for k in range(3)])
            mixes.append(tail[:mix_rows])

        band = (lax.axis_index("half") * rest + lax.axis_index("rest")).astype(jnp.int32)[None]
        member = (lax.axis_index("core") * rest + lax.axis_index("rest")).astype(jnp.int32)[None]
        sent = spread(memory[0], cut(channels // members, ENDS), members, band)
        last = len(sent) - 1

        def delivered(k, *waits):
            pieces = sent[k]
            if waits:
                pieces = lax.optimization_barrier((*pieces, *waits))[:members]
            return [lax.ppermute(piece, AXES, route) for piece, route in zip(pieces, spread_routes)]

        def later(values, *waits):
            return lax.optimization_barrier((*values, *waits))[: len(values)]

        sizes = [pieces[0].shape[0] for pieces in sent]
        starts = starts_of(sizes)

        def room(each, rows):
            return jax.ShapeDtypeStruct((members, 3, each, rows, width), jnp.bfloat16)

        full = [delivered(0, packs)]
        solved = [room(starts[last], height)]
        for k in range(last):
            waits = [*weights[0], *weights[1]] if k == 1 else earlier if k > 1 else []
            full.append(delivered(k + 1, *full[k], *waits))
            earlier = solved
            solved = relayed(full[k], member, *weights, solved, starts[k])
        ends = relayed(full[last], member, *weights, [room(sizes[last], ROW_TILE)] * row_chunks, 0)
        (solved,) = later(solved, *full[last])
        old = lax.ppermute(tied(memory[0].astype(jnp.bfloat16), *full[last]), AXES, shift_route)
        terms = [exchanged(solved.reshape(members, -1, height, width)).reshape(solved.shape)]
        terms[0], *solved = later([terms[0], *ends])
        solved = later(solved, old)

        out, rows = None, None
        moved = []
        for r in range(row_chunks):
            waits = ([rows] if r else []) + (moved[r - 2 : r - 1] if r > 1 else [])
            field = solved[r].reshape(members, -1, ROW_TILE, width)
            field = exchanged(tied(field, *waits) if waits else field)
            rows = finished(terms, field.reshape(solved[r].shape), mixes, r)
            ending = r > 1 and r == row_chunks - 1
            moved.append(lax.ppermute(tied(rows, moved[-1]) if ending else rows, AXES, return_route))
        for r in range(row_chunks):
            out = placed(moved[r], old, out, r, out_shape)
        return out[None]

    return jax.shard_map(
        on_device,
        mesh=fine,
        in_specs=(
            P(("lane", "core"), ("half", "rest"), None, None),
            P(("lane", "core"), None, None, None, None, None, None),
            P(("lane", "core"), None, None),
            P(("lane", "core"), None, None, None),
            P(("lane", "core"), None, None),
        ),
        out_specs=P(("lane", "core"), ("half", "rest"), None, None),
        check_vma=False,
    )
```

```python
import jax
import jax.numpy as jnp
from jax import lax
from jax.experimental import pallas as pl
from jax.experimental.pallas import tpu as pltpu
from jax.sharding import Mesh, PartitionSpec as P

TICKS = 2
ENDS = (6, 12, 16)
ROW_TILE = 16
PIECE = 512
AXES = ("lane", "core", "half", "rest")
GROUP = ("core", "rest")
VMEM = pltpu.CompilerParams(vmem_limit_bytes=58 << 20)


def cost(*arrays, products=0):
    size = sum(a.size * a.dtype.itemsize for a in arrays)
    return pl.CostEstimate(flops=2 * products, transcendentals=0, bytes_accessed=size)


def whole(shape):
    return pl.BlockSpec(shape, lambda *_: (0,) * len(shape))


def tied(value, *others):
    return lax.optimization_barrier((value, *others))[0]


def starts_of(sizes):
    return [sum(sizes[:k]) for k in range(len(sizes))]


def cut(count, ends):
    edges = [0] + [count * end // 16 for end in ends]
    return [high - low for low, high in zip(edges, edges[1:])]


def spread(memory, sizes, members, band):
    rows, width, channels = memory.shape
    each = channels // members
    starts = starts_of(sizes)

    def body(band_ref, source, *refs):
        outs, kept = refs[:-1], refs[-1]
        turned = jnp.transpose(source[...].astype(jnp.bfloat16), (2, 0, 1))
        kept[...] = turned.reshape(members, each, ROW_TILE, width)
        for c, (start, size) in enumerate(zip(starts, sizes)):
            for k in range(members):
                outs[c * members + k][...] = kept[band_ref[0] ^ k, start : start + size]

    pieces = [size for size in sizes for _ in range(members)]
    outs = pl.pallas_call(
        body,
        grid_spec=pltpu.PrefetchScalarGridSpec(
            num_scalar_prefetch=1,
            grid=(rows // ROW_TILE,),
            in_specs=[pl.BlockSpec((ROW_TILE, width, channels), lambda i, _: (i, 0, 0))],
            out_specs=[pl.BlockSpec((size, ROW_TILE, width), lambda i, _: (0, i, 0)) for size in pieces],
            scratch_shapes=[pltpu.VMEM((members, each, ROW_TILE, width), jnp.bfloat16)],
        ),
        out_shape=[jax.ShapeDtypeStruct((size, rows, width), jnp.bfloat16) for size in pieces],
        compiler_params=VMEM,
        cost_estimate=cost(memory, memory),
        name="spread",
    )(band, memory)
    return [outs[c * members : (c + 1) * members] for c in range(len(sizes))]


def packed(table, mixing):
    wide = mixing.shape[-1]
    numbers = table.reshape(-1).astype(jnp.bfloat16)
    short = -(-numbers.size // wide)
    short += -short % 16
    numbers = jnp.pad(numbers, (0, short * wide - numbers.size)).reshape(short, wide)
    return jnp.concatenate([mixing, numbers], axis=0)


def dense(blocks, table, which, shear, transposed):
    lines, outs_count, slots, wide = blocks.shape[2:6]
    size = outs_count * wide

    def body(table_ref, _, source, out):
        line = pl.program_id(0)
        out[...] = jnp.zeros(out.shape, out.dtype)
        for q in range(outs_count):
            for t in range(slots):
                place = table_ref[((shear * lines + line) * outs_count + q) * slots + t]
                start = pl.multiple_of(place * wide, wide)
                block = source[0, 0, 0, q, t]
                fixed = pl.ds(q * wide, wide)
                moved = pl.ds(start, wide)
                if transposed:
                    out[0, moved, fixed] += block.T
                else:
                    out[0, fixed, moved] += block

    return pl.pallas_call(
        body,
        grid_spec=pltpu.PrefetchScalarGridSpec(
            num_scalar_prefetch=2,
            grid=(lines,),
            in_specs=[
                pl.BlockSpec(
                    (1, 1, 1, outs_count, slots, wide, wide),
                    lambda i, _, which_ref: (which_ref[0], shear, i, 0, 0, 0, 0),
                )
            ],
            out_specs=pl.BlockSpec((1, size, size), lambda i, *_: (i, 0, 0)),
        ),
        out_shape=jax.ShapeDtypeStruct((lines, size, size), jnp.bfloat16),
        compiler_params=VMEM,
        cost_estimate=pl.CostEstimate(flops=0, transcendentals=0, bytes_accessed=8 * lines * size * size),
        name="dense",
    )(table, which, blocks)


def relayed(values, member, first, second, targets, start):
    row_chunks = len(targets)
    members = len(values)
    each, rows, width = values[0].shape
    lines = first[0].shape[0]
    wide = width // lines
    per = wide // rows
    pair = 2 if each % 2 == 0 and start % 2 == 0 else 1
    base = start // pair
    given = targets if start else []
    height = rows // row_chunks

    def body(member_ref, *refs):
        pieces, mats = refs[:members], refs[members : members + 6]
        outs, (source, kept, one, two) = refs[-4 - row_chunks : -4], refs[-4:]
        for k in range(members):
            source[member_ref[0] ^ k] = pieces[k][...]

        def shears(load, k, slots):
            for s in range(len(slots)):
                for i in range(lines):
                    got = jnp.dot(load(s, i), mats[3 * k][i], preferred_element_type=jnp.float32).astype(jnp.bfloat16)
                    for j in range(lines):
                        one[j, i * wide : (i + 1) * wide, s * wide : (s + 1) * wide] = got[:, j * wide : (j + 1) * wide]
            span = len(slots) * wide
            for j in range(lines):
                got = jnp.dot(mats[3 * k + 1][j], one[j, :, :span], preferred_element_type=jnp.float32)
                got = got.astype(jnp.bfloat16)
                for s in range(len(slots)):
                    two[s, :, j * wide : (j + 1) * wide] = got[:, s * wide : (s + 1) * wide]
            for s, (term, ch) in enumerate(slots):
                for i in range(lines):
                    lhs = two[s, i * wide : (i + 1) * wide]
                    got = jnp.dot(lhs, mats[3 * k + 2][i], preferred_element_type=jnp.float32).astype(jnp.bfloat16)
                    if term == 0:
                        kept[ch, i * wide : (i + 1) * wide] = got
                    split = got.reshape(per, row_chunks, height, width)
                    for r in range(row_chunks):
                        outs[r][per * i : per * (i + 1), term, ch] = split[:, r]

        def fresh(ch, i):
            return source[per * i : per * (i + 1), ch].reshape(wide, width)

        def held(s, i):
            if s < pair:
                return fresh(s, i)
            return kept[s - pair, i * wide : (i + 1) * wide]

        shears(fresh, 0, [(0, ch) for ch in range(pair)])
        shears(held, 1, [(term, ch) for term in (1, 2) for ch in range(pair)])

    mat = pl.BlockSpec(first[0].shape, lambda c, _: (0, 0, 0), pipeline_mode=pl.Buffered(1))
    return pl.pallas_call(
        body,
        grid_spec=pltpu.PrefetchScalarGridSpec(
            num_scalar_prefetch=1,
            grid=(each // pair,),
            in_specs=[pl.BlockSpec((pair, rows, width), lambda c, _: (c, 0, 0))] * members
            + [mat] * 6
            + [pl.BlockSpec(memory_space=pl.ANY)] * len(given),
            out_specs=[pl.BlockSpec((members, 3, pair, height, width), lambda c, _: (0, 0, base + c, 0, 0))] * row_chunks,
            scratch_shapes=[
                pltpu.VMEM((members, pair, rows, width), jnp.bfloat16),
                pltpu.VMEM((pair, width, width), jnp.bfloat16),
                pltpu.VMEM((lines, width, 2 * pair * wide), jnp.bfloat16),
                pltpu.VMEM((2 * pair, width, width), jnp.bfloat16),
            ],
        ),
        out_shape=[jax.ShapeDtypeStruct(target.shape, jnp.bfloat16) for target in targets],
        input_output_aliases={1 + members + 6 + r: r for r in range(len(given))},
        compiler_params=VMEM,
        cost_estimate=cost(*values * 4, *first, *second, products=18 * members * values[0].size * width),
        name="relayed",
    )(member, *values, *first, *second, *given)


def finished(terms, last, mixes, row_chunk):
    members, _, _, rows, width = last.shape
    channels = mixes[0].shape[0]
    piece = min(width, PIECE)
    count = len(terms) + 1

    def body(*refs):
        fields, one, two, out = refs[:count], refs[count][...], refs[count + 1][...], refs[count + 2]

        def by_row(pick):
            parts = [pick(j, k) for j in range(members) for k in range(count)]
            return jnp.swapaxes(jnp.concatenate(parts, axis=0), 0, 1)

        p, q, r = [by_row(lambda j, k: fields[k][j, term]) for term in range(3)]
        over_rows = (((0,), (0,)), ((), ()))
        for l in range(rows):
            both = jnp.concatenate([p[l], r[l]], axis=1)
            got = lax.dot_general(one, both, over_rows, preferred_element_type=jnp.float32)
            more = (q[l].astype(jnp.float32) + got[:, piece:]).astype(jnp.bfloat16)
            total = got[:, :piece] + lax.dot_general(two, more, over_rows, preferred_element_type=jnp.float32)
            out[l] = total.astype(jnp.bfloat16).T

    def term_block(a, at):
        return pl.BlockSpec((members, 3, a.shape[2], rows, piece), lambda i: (0, 0, 0, at, i))

    return pl.pallas_call(
        body,
        grid=(width // piece,),
        in_specs=[term_block(a, row_chunk) for a in terms]
        + [term_block(last, 0)]
        + [whole((channels, channels))] * 2,
        out_specs=pl.BlockSpec((rows, piece, channels), lambda i: (0, i, 0)),
        out_shape=jax.ShapeDtypeStruct((rows, width, channels), jnp.bfloat16),
        compiler_params=VMEM,
        cost_estimate=cost(last, last, last),
        name="finished",
    )(*terms, last, *mixes)


def placed(rows_in, old, target, row_chunk, shape):
    rows, width, channels = rows_in.shape
    piece = min(width, 128)

    def body(source, before, *refs):
        refs[-1][...] = before[...].astype(jnp.float32) + source[...].astype(jnp.float32)

    given = [] if target is None else [target]
    block = pl.BlockSpec((rows, piece, channels), lambda i: (0, i, 0))
    return pl.pallas_call(
        body,
        grid=(width // piece,),
        in_specs=[block, pl.BlockSpec((rows, piece, channels), lambda i: (row_chunk, i, 0))] + [pl.BlockSpec(memory_space=pl.ANY)] * len(given),
        out_specs=pl.BlockSpec((rows, piece, channels), lambda i: (row_chunk, i, 0)),
        out_shape=jax.ShapeDtypeStruct(shape, jnp.float32),
        input_output_aliases={2: 0} if given else {},
        compiler_params=VMEM,
        cost_estimate=cost(*[rows_in] * 5),
        name="placed",
    )(rows_in, old, *given)


def exchanged(values):
    return lax.all_to_all(values, GROUP, split_axis=0, concat_axis=0, tiled=True)


def solution(mesh):
    sections = mesh.shape["pipe"]
    bands = mesh.shape["band"]
    lanes, rest = sections // 2, bands // 2
    fine = Mesh(mesh.devices.reshape(lanes, 2, 2, rest), AXES)

    def flat(pipe, half, place):
        return (pipe * 2 + half) * rest + place

    places = [(pipe, band) for pipe in range(sections) for band in range(bands)]

    def at(pipe, band):
        return pipe * bands + band

    def hosts(section, member):
        return at(section // 2 * 2 + member // rest, section % 2 * rest + member % rest)

    spread_routes = [[(at(p, b), hosts(p, b ^ k)) for p, b in places] for k in range(bands)]
    pack_routes = [[(at((p + tick) % sections, b), hosts(p, b)) for p, b in places] for tick in range(TICKS)]
    shift_route = [(at(p, b), at((p + TICKS) % sections, b)) for p, b in places]
    return_route = [(hosts(p, b), at((p + TICKS) % sections, b)) for p, b in places]

    def on_device(memory, shear_blocks, shear_offsets, block_lists, mix_weight):
        line_count = shear_blocks.shape[2]
        source = (
            jnp.arange(line_count, dtype=jnp.int32)[None, None, :, None]
            + shear_offsets[0][:, :, None, None]
            + block_lists[0][:, None]
        ) % line_count
        pipe = ("lane", "core")
        own = lax.axis_index("lane") * 2 + lax.axis_index("half")
        all_blocks = lax.all_gather(shear_blocks[0], pipe)
        pack = packed(source, mix_weight[0])
        packs = [lax.ppermute(pack, AXES, route) for route in pack_routes]

        members, (_, height, width, channels) = bands, memory.shape
        row_chunks = height // ROW_TILE
        out_shape = memory.shape[1:]
        mix_rows = mix_weight.shape[1]
        weights, mixes = [], []
        for tick in range(TICKS):
            which = ((own + tick) % sections).astype(jnp.int32)[None]
            tail = packs[tick]
            table = tail[mix_rows:].reshape(-1)[: source.size].astype(jnp.int32)
            weights.append([dense(all_blocks, table, which, k, k != 1) for k in range(3)])
            mixes.append(tail[:mix_rows])

        band = (lax.axis_index("half") * rest + lax.axis_index("rest")).astype(jnp.int32)[None]
        member = (lax.axis_index("core") * rest + lax.axis_index("rest")).astype(jnp.int32)[None]
        sent = spread(memory[0], cut(channels // members, ENDS), members, band)
        last = len(sent) - 1

        def delivered(k, *waits):
            pieces = sent[k]
            if waits:
                pieces = lax.optimization_barrier((*pieces, *waits))[:members]
            return [lax.ppermute(piece, AXES, route) for piece, route in zip(pieces, spread_routes)]

        def later(values, *waits):
            return lax.optimization_barrier((*values, *waits))[: len(values)]

        sizes = [pieces[0].shape[0] for pieces in sent]
        starts = starts_of(sizes)

        def room(each, rows):
            return jax.ShapeDtypeStruct((members, 3, each, rows, width), jnp.bfloat16)

        full = [delivered(0, *packs)]
        solved = [room(starts[last], height)]
        for k in range(last):
            full.append(delivered(k + 1, *full[k], *(solved if k else [])))
            solved = relayed(full[k], member, *weights, solved, starts[k])
        ends = relayed(full[last], member, *weights, [room(sizes[last], ROW_TILE)] * row_chunks, 0)
        (solved,) = later(solved, *full[last])
        old = lax.ppermute(tied(memory[0].astype(jnp.bfloat16), *full[last]), AXES, shift_route)
        terms = [exchanged(solved.reshape(members, -1, height, width)).reshape(solved.shape)]
        terms[0], *solved = later([terms[0], *ends])
        solved = later(solved, old)

        out, rows = None, None
        moved = []
        for r in range(row_chunks):
            waits = ([rows] if r else []) + (moved[r - 2 : r - 1] if r > 1 else [])
            field = solved[r].reshape(members, -1, ROW_TILE, width)
            field = exchanged(tied(field, *waits) if waits else field)
            rows = finished(terms, field.reshape(solved[r].shape), mixes, r)
            ending = r > 1 and r == row_chunks - 1
            moved.append(lax.ppermute(tied(rows, moved[-1]) if ending else rows, AXES, return_route))
        for r in range(row_chunks):
            out = placed(moved[r], old, out, r, out_shape)
        return out[None]

    return jax.shard_map(
        on_device,
        mesh=fine,
        in_specs=(
            P(("lane", "core"), ("half", "rest"), None, None),
            P(("lane", "core"), None, None, None, None, None, None),
            P(("lane", "core"), None, None),
            P(("lane", "core"), None, None, None),
            P(("lane", "core"), None, None),
        ),
        out_specs=P(("lane", "core"), ("half", "rest"), None, None),
        check_vma=False,
    )
```

```python
import jax
import jax.numpy as jnp
from jax import lax
from jax.experimental import pallas as pl
from jax.experimental.pallas import tpu as pltpu
from jax.sharding import Mesh, PartitionSpec as P

TICKS = 2
ENDS = (6, 12, 16)
ROW_TILE = 16
PIECE = 256
AXES = ("lane", "core", "half", "rest")
GROUP = ("core", "rest")
VMEM = pltpu.CompilerParams(vmem_limit_bytes=58 << 20)


def cost(*arrays, products=0):
    size = sum(a.size * a.dtype.itemsize for a in arrays)
    return pl.CostEstimate(flops=2 * products, transcendentals=0, bytes_accessed=size)


def whole(shape):
    return pl.BlockSpec(shape, lambda *_: (0,) * len(shape))


def tied(value, *others):
    return lax.optimization_barrier((value, *others))[0]


def starts_of(sizes):
    return [sum(sizes[:k]) for k in range(len(sizes))]


def cut(count, ends):
    edges = [0] + [count * end // 16 for end in ends]
    return [high - low for low, high in zip(edges, edges[1:])]


def spread(memory, sizes, members, band):
    rows, width, channels = memory.shape
    each = channels // members
    starts = starts_of(sizes)

    def body(band_ref, source, *refs):
        outs, kept = refs[:-1], refs[-1]
        turned = jnp.transpose(source[...].astype(jnp.bfloat16), (2, 0, 1))
        kept[...] = turned.reshape(members, each, ROW_TILE, width)
        for c, (start, size) in enumerate(zip(starts, sizes)):
            for k in range(members):
                outs[c * members + k][...] = kept[band_ref[0] ^ k, start : start + size]

    pieces = [size for size in sizes for _ in range(members)]
    outs = pl.pallas_call(
        body,
        grid_spec=pltpu.PrefetchScalarGridSpec(
            num_scalar_prefetch=1,
            grid=(rows // ROW_TILE,),
            in_specs=[pl.BlockSpec((ROW_TILE, width, channels), lambda i, _: (i, 0, 0))],
            out_specs=[pl.BlockSpec((size, ROW_TILE, width), lambda i, _: (0, i, 0)) for size in pieces],
            scratch_shapes=[pltpu.VMEM((members, each, ROW_TILE, width), jnp.bfloat16)],
        ),
        out_shape=[jax.ShapeDtypeStruct((size, rows, width), jnp.bfloat16) for size in pieces],
        compiler_params=VMEM,
        cost_estimate=cost(memory, memory),
        name="spread",
    )(band, memory)
    return [outs[c * members : (c + 1) * members] for c in range(len(sizes))]


def packed(table, mixing):
    wide = mixing.shape[-1]
    numbers = table.reshape(-1).astype(jnp.bfloat16)
    short = -(-numbers.size // wide)
    short += -short % 16
    numbers = jnp.pad(numbers, (0, short * wide - numbers.size)).reshape(short, wide)
    return jnp.concatenate([mixing, numbers], axis=0)


def dense(blocks, table, which, shear, transposed):
    lines, outs_count, slots, wide = blocks.shape[2:6]
    size = outs_count * wide

    def body(table_ref, _, source, out):
        line = pl.program_id(0)
        out[...] = jnp.zeros(out.shape, out.dtype)

        @pl.loop(0, outs_count)
        def _(q):
            fixed = pl.ds(pl.multiple_of(q * wide, wide), wide)
            for t in range(slots):
                place = table_ref[((shear * lines + line) * outs_count + q) * slots + t]
                moved = pl.ds(pl.multiple_of(place * wide, wide), wide)
                block = source[0, 0, 0, q, t]
                if transposed:
                    out[0, moved, fixed] += block.T
                else:
                    out[0, fixed, moved] += block

    return pl.pallas_call(
        body,
        grid_spec=pltpu.PrefetchScalarGridSpec(
            num_scalar_prefetch=2,
            grid=(lines,),
            in_specs=[
                pl.BlockSpec(
                    (1, 1, 1, outs_count, slots, wide, wide),
                    lambda i, _, which_ref: (which_ref[0], shear, i, 0, 0, 0, 0),
                )
            ],
            out_specs=pl.BlockSpec((1, size, size), lambda i, *_: (i, 0, 0)),
        ),
        out_shape=jax.ShapeDtypeStruct((lines, size, size), jnp.bfloat16),
        compiler_params=VMEM,
        cost_estimate=pl.CostEstimate(flops=0, transcendentals=0, bytes_accessed=8 * lines * size * size),
        name="dense",
    )(table, which, blocks)


def relayed(values, member, first, second, targets, start, compact=False):
    row_chunks = len(targets)
    members = len(values)
    each, rows, width = values[0].shape
    lines = first[0].shape[0]
    wide = width // lines
    per = wide // rows
    pair = 2 if each % 2 == 0 and start % 2 == 0 else 1
    base = start // pair
    given = targets if start else []
    height = rows // row_chunks

    def body(member_ref, *refs):
        pieces, mats = refs[:members], refs[members : members + 6]
        outs, (source, kept, one, two) = refs[-4 - row_chunks : -4], refs[-4:]
        for k in range(members):
            source[member_ref[0] ^ k] = pieces[k][...]

        def rows_of(i):
            return pl.ds(pl.multiple_of(i * wide, wide) if compact else i * wide, wide)

        def over_lines(step):
            if compact:
                pl.loop(0, lines)(step)
            else:
                for i in range(lines):
                    step(i)

        def shears(load, k, slots):
            for s in range(len(slots)):

                @over_lines
                def _(i):
                    got = jnp.dot(load(s, i), mats[3 * k][i], preferred_element_type=jnp.float32).astype(jnp.bfloat16)
                    at_rows = rows_of(i)
                    for j in range(lines):
                        one[j, at_rows, s * wide : (s + 1) * wide] = got[:, j * wide : (j + 1) * wide]

            span = len(slots) * wide
            for j in range(lines):
                got = jnp.dot(mats[3 * k + 1][j], one[j, :, :span], preferred_element_type=jnp.float32)
                got = got.astype(jnp.bfloat16)
                for s in range(len(slots)):
                    two[s, :, j * wide : (j + 1) * wide] = got[:, s * wide : (s + 1) * wide]
            for s, (term, ch) in enumerate(slots):

                @over_lines
                def _(i):
                    at_rows = rows_of(i)
                    lhs = two[s, at_rows]
                    got = jnp.dot(lhs, mats[3 * k + 2][i], preferred_element_type=jnp.float32).astype(jnp.bfloat16)
                    if term == 0:
                        kept[ch, at_rows] = got
                    split = got.reshape(per, row_chunks, height, width)
                    for r in range(row_chunks):
                        outs[r][pl.ds(per * i, per), term, ch] = split[:, r]

        def fresh(ch, i):
            return source[pl.ds(per * i, per), ch].reshape(wide, width)

        def held(s, i):
            if s < pair:
                return fresh(s, i)
            return kept[s - pair, rows_of(i)]

        shears(fresh, 0, [(0, ch) for ch in range(pair)])
        shears(held, 1, [(term, ch) for term in (1, 2) for ch in range(pair)])

    mat = pl.BlockSpec(first[0].shape, lambda c, _: (0, 0, 0), pipeline_mode=pl.Buffered(1))
    return pl.pallas_call(
        body,
        grid_spec=pltpu.PrefetchScalarGridSpec(
            num_scalar_prefetch=1,
            grid=(each // pair,),
            in_specs=[pl.BlockSpec((pair, rows, width), lambda c, _: (c, 0, 0))] * members
            + [mat] * 6
            + [pl.BlockSpec(memory_space=pl.ANY)] * len(given),
            out_specs=[pl.BlockSpec((members, 3, pair, height, width), lambda c, _: (0, 0, base + c, 0, 0))] * row_chunks,
            scratch_shapes=[
                pltpu.VMEM((members, pair, rows, width), jnp.bfloat16),
                pltpu.VMEM((pair, width, width), jnp.bfloat16),
                pltpu.VMEM((lines, width, 2 * pair * wide), jnp.bfloat16),
                pltpu.VMEM((2 * pair, width, width), jnp.bfloat16),
            ],
        ),
        out_shape=[jax.ShapeDtypeStruct(target.shape, jnp.bfloat16) for target in targets],
        input_output_aliases={1 + members + 6 + r: r for r in range(len(given))},
        compiler_params=VMEM,
        cost_estimate=cost(*values * 4, *first, *second, products=18 * members * values[0].size * width),
        name="relayed",
    )(member, *values, *first, *second, *given)


def finished(terms, last, mixes, row_chunk):
    members, _, _, rows, width = last.shape
    channels = mixes[0].shape[0]
    piece = min(width, PIECE)
    count = len(terms) + 1

    def body(*refs):
        fields, one, two, out = refs[:count], refs[count][...], refs[count + 1][...], refs[count + 2]

        def by_row(pick):
            parts = [pick(j, k) for j in range(members) for k in range(count)]
            return jnp.swapaxes(jnp.concatenate(parts, axis=0), 0, 1)

        p, q, r = [by_row(lambda j, k: fields[k][j, term]) for term in range(3)]
        over_rows = (((0,), (0,)), ((), ()))
        for l in range(rows):
            both = jnp.concatenate([p[l], r[l]], axis=1)
            got = lax.dot_general(one, both, over_rows, preferred_element_type=jnp.float32)
            more = (q[l].astype(jnp.float32) + got[:, piece:]).astype(jnp.bfloat16)
            total = got[:, :piece] + lax.dot_general(two, more, over_rows, preferred_element_type=jnp.float32)
            out[l] = total.astype(jnp.bfloat16).T

    def term_block(a, at):
        return pl.BlockSpec((members, 3, a.shape[2], rows, piece), lambda i: (0, 0, 0, at, i))

    return pl.pallas_call(
        body,
        grid=(width // piece,),
        in_specs=[term_block(a, row_chunk) for a in terms]
        + [term_block(last, 0)]
        + [whole((channels, channels))] * 2,
        out_specs=pl.BlockSpec((rows, piece, channels), lambda i: (0, i, 0)),
        out_shape=jax.ShapeDtypeStruct((rows, width, channels), jnp.bfloat16),
        compiler_params=VMEM,
        cost_estimate=cost(last, last, last),
        name="finished",
    )(*terms, last, *mixes)


def placed(rows_in, old, target, row_chunk, shape):
    rows, width, channels = rows_in.shape
    piece = min(width, 128)

    def body(source, before, *refs):
        refs[-1][...] = before[...].astype(jnp.float32) + source[...].astype(jnp.float32)

    given = [] if target is None else [target]
    block = pl.BlockSpec((rows, piece, channels), lambda i: (0, i, 0))
    return pl.pallas_call(
        body,
        grid=(width // piece,),
        in_specs=[block, pl.BlockSpec((rows, piece, channels), lambda i: (row_chunk, i, 0))] + [pl.BlockSpec(memory_space=pl.ANY)] * len(given),
        out_specs=pl.BlockSpec((rows, piece, channels), lambda i: (row_chunk, i, 0)),
        out_shape=jax.ShapeDtypeStruct(shape, jnp.float32),
        input_output_aliases={2: 0} if given else {},
        compiler_params=VMEM,
        cost_estimate=cost(*[rows_in] * 5),
        name="placed",
    )(rows_in, old, *given)


def exchanged(values):
    return lax.all_to_all(values, GROUP, split_axis=0, concat_axis=0, tiled=True)


def solution(mesh):
    sections = mesh.shape["pipe"]
    bands = mesh.shape["band"]
    lanes, rest = sections // 2, bands // 2
    fine = Mesh(mesh.devices.reshape(lanes, 2, 2, rest), AXES)

    def flat(pipe, half, place):
        return (pipe * 2 + half) * rest + place

    places = [(pipe, band) for pipe in range(sections) for band in range(bands)]

    def at(pipe, band):
        return pipe * bands + band

    def hosts(section, member):
        return at(section // 2 * 2 + member // rest, section % 2 * rest + member % rest)

    spread_routes = [[(at(p, b), hosts(p, b ^ k)) for p, b in places] for k in range(bands)]
    pack_routes = [[(at((p + tick) % sections, b), hosts(p, b)) for p, b in places] for tick in range(TICKS)]
    shift_route = [(at(p, b), at((p + TICKS) % sections, b)) for p, b in places]
    return_route = [(hosts(p, b), at((p + TICKS) % sections, b)) for p, b in places]

    def on_device(memory, shear_blocks, shear_offsets, block_lists, mix_weight):
        line_count = shear_blocks.shape[2]
        source = (
            jnp.arange(line_count, dtype=jnp.int32)[None, None, :, None]
            + shear_offsets[0][:, :, None, None]
            + block_lists[0][:, None]
        ) % line_count
        pipe = ("lane", "core")
        own = lax.axis_index("lane") * 2 + lax.axis_index("half")
        all_blocks = lax.all_gather(shear_blocks[0], pipe)
        pack = packed(source, mix_weight[0])
        packs = [lax.ppermute(pack, AXES, route) for route in pack_routes]

        members, (_, height, width, channels) = bands, memory.shape
        row_chunks = height // ROW_TILE
        out_shape = memory.shape[1:]
        mix_rows = mix_weight.shape[1]
        weights, mixes = [], []
        for tick in range(TICKS):
            which = ((own + tick) % sections).astype(jnp.int32)[None]
            tail = packs[tick]
            table = tail[mix_rows:].reshape(-1)[: source.size].astype(jnp.int32)
            weights.append([dense(all_blocks, table, which, k, k != 1) for k in range(3)])
            mixes.append(tail[:mix_rows])

        band = (lax.axis_index("half") * rest + lax.axis_index("rest")).astype(jnp.int32)[None]
        member = (lax.axis_index("core") * rest + lax.axis_index("rest")).astype(jnp.int32)[None]
        sent = spread(memory[0], cut(channels // members, ENDS), members, band)
        last = len(sent) - 1

        def delivered(k, *waits):
            pieces = sent[k]
            if waits:
                pieces = lax.optimization_barrier((*pieces, *waits))[:members]
            return [lax.ppermute(piece, AXES, route) for piece, route in zip(pieces, spread_routes)]

        def later(values, *waits):
            return lax.optimization_barrier((*values, *waits))[: len(values)]

        sizes = [pieces[0].shape[0] for pieces in sent]
        starts = starts_of(sizes)

        def room(each, rows):
            return jax.ShapeDtypeStruct((members, 3, each, rows, width), jnp.bfloat16)

        full = [delivered(0, *packs)]
        solved = [room(starts[last], height)]
        for k in range(last):
            full.append(delivered(k + 1, *full[k], *(solved if k else [])))
            solved = relayed(full[k], member, *weights, solved, starts[k])
        ends = relayed(full[last], member, *weights, [room(sizes[last], ROW_TILE)] * row_chunks, 0, compact=True)
        (solved,) = later(solved, *full[last])
        old = lax.ppermute(tied(memory[0].astype(jnp.bfloat16), *full[last]), AXES, shift_route)
        terms = [exchanged(solved.reshape(members, -1, height, width)).reshape(solved.shape)]
        terms[0], *solved = later([terms[0], *ends])
        solved = later(solved, old)

        out, rows = None, None
        moved = []
        for r in range(row_chunks):
            waits = ([rows] if r else []) + (moved[r - 2 : r - 1] if r > 1 else [])
            field = solved[r].reshape(members, -1, ROW_TILE, width)
            field = exchanged(tied(field, *waits) if waits else field)
            rows = finished(terms, field.reshape(solved[r].shape), mixes, r)
            ending = r > 1 and r == row_chunks - 1
            moved.append(lax.ppermute(tied(rows, moved[-1]) if ending else rows, AXES, return_route))
        for r in range(row_chunks):
            out = placed(moved[r], old, out, r, out_shape)
        return out[None]

    return jax.shard_map(
        on_device,
        mesh=fine,
        in_specs=(
            P(("lane", "core"), ("half", "rest"), None, None),
            P(("lane", "core"), None, None, None, None, None, None),
            P(("lane", "core"), None, None),
            P(("lane", "core"), None, None, None),
            P(("lane", "core"), None, None),
        ),
        out_specs=P(("lane", "core"), ("half", "rest"), None, None),
        check_vma=False,
    )
```

```python
import jax
import jax.numpy as jnp
from jax import lax
from jax.experimental import pallas as pl
from jax.experimental.pallas import tpu as pltpu
from jax.sharding import Mesh, PartitionSpec as P

TICKS = 2
ENDS = (6, 12, 16)
ROW_TILE = 16
PIECE = 256
AXES = ("lane", "core", "half", "rest")
GROUP = ("core", "rest")
VMEM = pltpu.CompilerParams(vmem_limit_bytes=58 << 20)


def cost(*arrays, products=0):
    size = sum(a.size * a.dtype.itemsize for a in arrays)
    return pl.CostEstimate(flops=2 * products, transcendentals=0, bytes_accessed=size)


def whole(shape):
    return pl.BlockSpec(shape, lambda *_: (0,) * len(shape))


def tied(value, *others):
    return lax.optimization_barrier((value, *others))[0]


def starts_of(sizes):
    return [sum(sizes[:k]) for k in range(len(sizes))]


def cut(count, ends):
    edges = [0] + [count * end // 16 for end in ends]
    return [high - low for low, high in zip(edges, edges[1:])]


def spread(memory, sizes, members, band):
    rows, width, channels = memory.shape
    each = channels // members
    starts = starts_of(sizes)

    def body(band_ref, source, *refs):
        outs, kept = refs[:-1], refs[-1]
        turned = jnp.transpose(source[...].astype(jnp.bfloat16), (2, 0, 1))
        kept[...] = turned.reshape(members, each, ROW_TILE, width)
        for c, (start, size) in enumerate(zip(starts, sizes)):
            for k in range(members):
                outs[c * members + k][...] = kept[band_ref[0] ^ k, start : start + size]

    pieces = [size for size in sizes for _ in range(members)]
    outs = pl.pallas_call(
        body,
        grid_spec=pltpu.PrefetchScalarGridSpec(
            num_scalar_prefetch=1,
            grid=(rows // ROW_TILE,),
            in_specs=[pl.BlockSpec((ROW_TILE, width, channels), lambda i, _: (i, 0, 0))],
            out_specs=[pl.BlockSpec((size, ROW_TILE, width), lambda i, _: (0, i, 0)) for size in pieces],
            scratch_shapes=[pltpu.VMEM((members, each, ROW_TILE, width), jnp.bfloat16)],
        ),
        out_shape=[jax.ShapeDtypeStruct((size, rows, width), jnp.bfloat16) for size in pieces],
        compiler_params=VMEM,
        cost_estimate=cost(memory, memory),
        name="spread",
    )(band, memory)
    return [outs[c * members : (c + 1) * members] for c in range(len(sizes))]


def packed(table, mixing):
    wide = mixing.shape[-1]
    numbers = table.reshape(-1).astype(jnp.bfloat16)
    short = -(-numbers.size // wide)
    short += -short % 16
    numbers = jnp.pad(numbers, (0, short * wide - numbers.size)).reshape(short, wide)
    return jnp.concatenate([mixing, numbers], axis=0)


def dense(blocks, table, which, shear, transposed):
    lines, outs_count, slots, wide = blocks.shape[2:6]
    size = outs_count * wide

    def body(table_ref, _, source, out):
        line = pl.program_id(0)
        out[...] = jnp.zeros(out.shape, out.dtype)

        @pl.loop(0, outs_count)
        def _(q):
            fixed = pl.ds(pl.multiple_of(q * wide, wide), wide)
            for t in range(slots):
                place = table_ref[((shear * lines + line) * outs_count + q) * slots + t]
                moved = pl.ds(pl.multiple_of(place * wide, wide), wide)
                block = source[0, 0, 0, q, t]
                if transposed:
                    out[0, moved, fixed] += block.T
                else:
                    out[0, fixed, moved] += block

    return pl.pallas_call(
        body,
        grid_spec=pltpu.PrefetchScalarGridSpec(
            num_scalar_prefetch=2,
            grid=(lines,),
            in_specs=[
                pl.BlockSpec(
                    (1, 1, 1, outs_count, slots, wide, wide),
                    lambda i, _, which_ref: (which_ref[0], shear, i, 0, 0, 0, 0),
                )
            ],
            out_specs=pl.BlockSpec((1, size, size), lambda i, *_: (i, 0, 0)),
        ),
        out_shape=jax.ShapeDtypeStruct((lines, size, size), jnp.bfloat16),
        compiler_params=VMEM,
        cost_estimate=pl.CostEstimate(flops=0, transcendentals=0, bytes_accessed=8 * lines * size * size),
        name="dense",
    )(table, which, blocks)


def relayed(values, member, first, second, targets, start, compact=False):
    row_chunks = len(targets)
    members = len(values)
    each, rows, width = values[0].shape
    lines = first[0].shape[0]
    wide = width // lines
    per = wide // rows
    pair = 2 if each % 2 == 0 and start % 2 == 0 else 1
    base = start // pair
    given = targets if start else []
    height = rows // row_chunks

    def body(member_ref, *refs):
        pieces, mats = refs[:members], refs[members : members + 6]
        outs, (source, kept, one, two) = refs[-4 - row_chunks : -4], refs[-4:]
        for k in range(members):
            source[member_ref[0] ^ k] = pieces[k][...]

        def rows_of(i):
            return pl.ds(pl.multiple_of(i * wide, wide) if compact else i * wide, wide)

        def over_lines(step):
            if compact:
                pl.loop(0, lines)(step)
            else:
                for i in range(lines):
                    step(i)

        def shears(load, k, slots):
            for s in range(len(slots)):

                @over_lines
                def _(i):
                    got = jnp.dot(load(s, i), mats[3 * k][i], preferred_element_type=jnp.float32).astype(jnp.bfloat16)
                    at_rows = rows_of(i)
                    for j in range(lines):
                        one[j, at_rows, s * wide : (s + 1) * wide] = got[:, j * wide : (j + 1) * wide]

            span = len(slots) * wide
            for j in range(lines):
                got = jnp.dot(mats[3 * k + 1][j], one[j, :, :span], preferred_element_type=jnp.float32)
                got = got.astype(jnp.bfloat16)
                for s in range(len(slots)):
                    two[s, :, j * wide : (j + 1) * wide] = got[:, s * wide : (s + 1) * wide]
            for s, (term, ch) in enumerate(slots):

                @over_lines
                def _(i):
                    at_rows = rows_of(i)
                    lhs = two[s, at_rows]
                    got = jnp.dot(lhs, mats[3 * k + 2][i], preferred_element_type=jnp.float32).astype(jnp.bfloat16)
                    if term == 0:
                        kept[ch, at_rows] = got
                    split = got.reshape(per, row_chunks, height, width)
                    for r in range(row_chunks):
                        outs[r][pl.ds(per * i, per), term, ch] = split[:, r]

        def fresh(ch, i):
            return source[pl.ds(per * i, per), ch].reshape(wide, width)

        def held(s, i):
            if s < pair:
                return fresh(s, i)
            return kept[s - pair, rows_of(i)]

        shears(fresh, 0, [(0, ch) for ch in range(pair)])
        shears(held, 1, [(term, ch) for term in (1, 2) for ch in range(pair)])

    mat = pl.BlockSpec(first[0].shape, lambda c, _: (0, 0, 0), pipeline_mode=pl.Buffered(1))
    return pl.pallas_call(
        body,
        grid_spec=pltpu.PrefetchScalarGridSpec(
            num_scalar_prefetch=1,
            grid=(each // pair,),
            in_specs=[pl.BlockSpec((pair, rows, width), lambda c, _: (c, 0, 0))] * members
            + [mat] * 6
            + [pl.BlockSpec(memory_space=pl.ANY)] * len(given),
            out_specs=[pl.BlockSpec((members, 3, pair, height, width), lambda c, _: (0, 0, base + c, 0, 0))] * row_chunks,
            scratch_shapes=[
                pltpu.VMEM((members, pair, rows, width), jnp.bfloat16),
                pltpu.VMEM((pair, width, width), jnp.bfloat16),
                pltpu.VMEM((lines, width, 2 * pair * wide), jnp.bfloat16),
                pltpu.VMEM((2 * pair, width, width), jnp.bfloat16),
            ],
        ),
        out_shape=[jax.ShapeDtypeStruct(target.shape, jnp.bfloat16) for target in targets],
        input_output_aliases={1 + members + 6 + r: r for r in range(len(given))},
        compiler_params=VMEM,
        cost_estimate=cost(*values * 4, *first, *second, products=18 * members * values[0].size * width),
        name="relayed",
    )(member, *values, *first, *second, *given)


def finished(terms, last, mixes, row_chunk):
    members, _, _, rows, width = last.shape
    channels = mixes[0].shape[0]
    piece = min(width, PIECE)
    count = len(terms) + 1

    def body(*refs):
        fields, one, two, out = refs[:count], refs[count][...], refs[count + 1][...], refs[count + 2]

        def by_row(pick):
            parts = [pick(j, k) for j in range(members) for k in range(count)]
            return jnp.swapaxes(jnp.concatenate(parts, axis=0), 0, 1)

        p, q, r = [by_row(lambda j, k: fields[k][j, term]) for term in range(3)]
        over_rows = (((0,), (0,)), ((), ()))
        for l in range(rows):
            both = jnp.concatenate([p[l], r[l]], axis=1)
            got = lax.dot_general(one, both, over_rows, preferred_element_type=jnp.float32)
            more = (q[l].astype(jnp.float32) + got[:, piece:]).astype(jnp.bfloat16)
            total = got[:, :piece] + lax.dot_general(two, more, over_rows, preferred_element_type=jnp.float32)
            out[l] = total.astype(jnp.bfloat16).T

    def term_block(a, at):
        return pl.BlockSpec((members, 3, a.shape[2], rows, piece), lambda i: (0, 0, 0, at, i))

    return pl.pallas_call(
        body,
        grid=(width // piece,),
        in_specs=[term_block(a, row_chunk) for a in terms]
        + [term_block(last, 0)]
        + [whole((channels, channels))] * 2,
        out_specs=pl.BlockSpec((rows, piece, channels), lambda i: (0, i, 0)),
        out_shape=jax.ShapeDtypeStruct((rows, width, channels), jnp.bfloat16),
        compiler_params=VMEM,
        cost_estimate=cost(last, last, last),
        name="finished",
    )(*terms, last, *mixes)


def placed(rows_in, old, target, row_chunk, shape):
    rows, width, channels = rows_in.shape
    piece = min(width, PIECE)

    def body(source, before, *refs):
        refs[-1][...] = before[...].astype(jnp.float32) + source[...].astype(jnp.float32)

    given = [] if target is None else [target]
    block = pl.BlockSpec((rows, piece, channels), lambda i: (0, i, 0))
    return pl.pallas_call(
        body,
        grid=(width // piece,),
        in_specs=[block, pl.BlockSpec((rows, piece, channels), lambda i: (row_chunk, i, 0))] + [pl.BlockSpec(memory_space=pl.ANY)] * len(given),
        out_specs=pl.BlockSpec((rows, piece, channels), lambda i: (row_chunk, i, 0)),
        out_shape=jax.ShapeDtypeStruct(shape, jnp.float32),
        input_output_aliases={2: 0} if given else {},
        compiler_params=VMEM,
        cost_estimate=cost(*[rows_in] * 5),
        name="placed",
    )(rows_in, old, *given)


def exchanged(values):
    return lax.all_to_all(values, GROUP, split_axis=0, concat_axis=0, tiled=True)


def solution(mesh):
    sections = mesh.shape["pipe"]
    bands = mesh.shape["band"]
    lanes, rest = sections // 2, bands // 2
    fine = Mesh(mesh.devices.reshape(lanes, 2, 2, rest), AXES)

    def flat(pipe, half, place):
        return (pipe * 2 + half) * rest + place

    places = [(pipe, band) for pipe in range(sections) for band in range(bands)]

    def at(pipe, band):
        return pipe * bands + band

    def hosts(section, member):
        return at(section // 2 * 2 + member // rest, section % 2 * rest + member % rest)

    spread_routes = [[(at(p, b), hosts(p, b ^ k)) for p, b in places] for k in range(bands)]
    pack_routes = [[(at((p + tick) % sections, b), hosts(p, b)) for p, b in places] for tick in range(TICKS)]
    shift_route = [(at(p, b), at((p + TICKS) % sections, b)) for p, b in places]
    return_route = [(hosts(p, b), at((p + TICKS) % sections, b)) for p, b in places]

    def on_device(memory, shear_blocks, shear_offsets, block_lists, mix_weight):
        line_count = shear_blocks.shape[2]
        source = (
            jnp.arange(line_count, dtype=jnp.int32)[None, None, :, None]
            + shear_offsets[0][:, :, None, None]
            + block_lists[0][:, None]
        ) % line_count
        pipe = ("lane", "core")
        own = lax.axis_index("lane") * 2 + lax.axis_index("half")
        all_blocks = lax.all_gather(shear_blocks[0], pipe)
        pack = packed(source, mix_weight[0])
        packs = [lax.ppermute(pack, AXES, route) for route in pack_routes]

        members, (_, height, width, channels) = bands, memory.shape
        row_chunks = height // ROW_TILE
        out_shape = memory.shape[1:]
        mix_rows = mix_weight.shape[1]
        weights, mixes = [], []
        for tick in range(TICKS):
            which = ((own + tick) % sections).astype(jnp.int32)[None]
            tail = packs[tick]
            table = tail[mix_rows:].reshape(-1)[: source.size].astype(jnp.int32)
            weights.append([dense(all_blocks, table, which, k, k != 1) for k in range(3)])
            mixes.append(tail[:mix_rows])

        band = (lax.axis_index("half") * rest + lax.axis_index("rest")).astype(jnp.int32)[None]
        member = (lax.axis_index("core") * rest + lax.axis_index("rest")).astype(jnp.int32)[None]
        sent = spread(memory[0], cut(channels // members, ENDS), members, band)
        last = len(sent) - 1

        def delivered(k, *waits):
            pieces = sent[k]
            if waits:
                pieces = lax.optimization_barrier((*pieces, *waits))[:members]
            return [lax.ppermute(piece, AXES, route) for piece, route in zip(pieces, spread_routes)]

        def later(values, *waits):
            return lax.optimization_barrier((*values, *waits))[: len(values)]

        sizes = [pieces[0].shape[0] for pieces in sent]
        starts = starts_of(sizes)

        def room(each, rows):
            return jax.ShapeDtypeStruct((members, 3, each, rows, width), jnp.bfloat16)

        full = [delivered(0, *packs)]
        solved = [room(starts[last], height)]
        for k in range(last):
            full.append(delivered(k + 1, *full[k], *(solved if k else [])))
            solved = relayed(full[k], member, *weights, solved, starts[k])
        ends = relayed(full[last], member, *weights, [room(sizes[last], ROW_TILE)] * row_chunks, 0, compact=True)
        (solved,) = later(solved, *full[last])
        old = lax.ppermute(tied(memory[0].astype(jnp.bfloat16), *full[last]), AXES, shift_route)
        terms = [exchanged(solved.reshape(members, -1, height, width)).reshape(solved.shape)]
        terms[0], *solved = later([terms[0], *ends])
        solved = later(solved, old)

        out, rows = None, None
        moved = []
        for r in range(row_chunks):
            waits = ([rows] if r else []) + (moved[r - 2 : r - 1] if r > 1 else [])
            field = solved[r].reshape(members, -1, ROW_TILE, width)
            field = exchanged(tied(field, *waits) if waits else field)
            rows = finished(terms, field.reshape(solved[r].shape), mixes, r)
            ending = r > 1 and r == row_chunks - 1
            moved.append(lax.ppermute(tied(rows, moved[-1]) if ending else rows, AXES, return_route))
        for r in range(row_chunks):
            out = placed(moved[r], old, out, r, out_shape)
        return out[None]

    return jax.shard_map(
        on_device,
        mesh=fine,
        in_specs=(
            P(("lane", "core"), ("half", "rest"), None, None),
            P(("lane", "core"), None, None, None, None, None, None),
            P(("lane", "core"), None, None),
            P(("lane", "core"), None, None, None),
            P(("lane", "core"), None, None),
        ),
        out_specs=P(("lane", "core"), ("half", "rest"), None, None),
        check_vma=False,
    )
```
